32 devices in a mesh: section: 2 (over x), dp: 4 (over z), mp: 4 (over y, core).
Axes of the slice: x: 2, y: 2, z: 4, core: 2. Of those that a mesh axis runs over, the one named last changes fastest.
Arguments:
- hidden: bfloat16 [2, 512, 4096], P('section', 'dp'), may hold values from -9 to 9
- norm_gain: float32 [2, 4096], P('section'), may hold values from 0.5 to 1.5
- kv_weight: bfloat16 [2, 4096, 2048], P('section', None, 'mp'), may hold values from -1 to 1
- attn_flat: bfloat16 [2, 4, 8388608], P('section', 'mp', 'dp'), may hold values from -1 to 1
- final_gain: float32 [4096], replicated, may hold values from 0.5 to 1.5
- reward_head: float32 [4096], replicated, may hold values from -0.09375 to 0.09375
- segment_ids: int32 [2, 4], P('section'), may hold values from 0 to 2, never falling along the last dimension, each value on 1 to 2 neighbouring positions
- ranks: int32 [2], replicated, may hold values from 0 to 999
Outputs:
- next_hidden: bfloat16 [2, 512, 4096], P('section', 'dp')
- rewards: float32 [2], replicated
- pair_loss: float32 [2, 2], replicated
The draws below stay inside these ranges and needn't reach their ends.
Inputs may be any that keep to these rules, and one draw needn't show every extreme that they name: `segment_ids`: each row's segment numbers never fall, every number of 0 to 2 is present, each on 1 to 2 blocks, one on exactly 2.
All inputs are finite; a program needn't handle non-finite values.
Results may differ from the reference program's by a relative error of at most 0.035.
Values may be sent and summed in bfloat16 or wider, within the bound.
A program may use at most 128 MiB of HBM per device.

```python
import math
import jax
import jax.numpy as jnp
import numpy as np
from jax import lax

D = 4096
HD = 128
QH = 32
KVH = 8
BLK = 128
L = 512
R = 2
MOST = 2
SHARD = 2097152
N_SECTION = 2
N_DP = 4
N_MP = 4


def plant_signs(key):
    shared = jax.random.fold_in(key, 7001)
    sign_key = jax.random.fold_in(shared, 1)
    head_key = jax.random.fold_in(shared, 2)
    direction = (2 * jax.random.randint(sign_key, (D,), 0, 2) - 1).astype(jnp.float32)
    pattern = (2 * jax.random.randint(head_key, (HD,), 0, 2) - 1).astype(jnp.float32)
    return (direction, pattern)


def plant_strength():
    return (332.4 / (D * D * HD ** 0.5)) ** 0.5


def draw_hidden(key, part):
    direction, pattern = plant_signs(key)
    noise_key = jax.random.fold_in(key, 11)
    pick_key = jax.random.fold_in(key, 12)
    level_key = jax.random.fold_in(key, 13)
    first_key = jax.random.fold_in(key, 14)
    full_shape = (N_SECTION, L, D)
    noise_part = jax.random.truncated_normal(noise_key, -6.0, 6.0, full_shape, jnp.float32)
    chance = jax.random.randint(pick_key, (N_SECTION, L), 0, 16)
    position = jnp.arange(L, dtype=jnp.int32)
    in_first = (position < BLK)[None, :]
    forced = position[None, :] == jax.random.randint(first_key, (N_SECTION, 1), 0, BLK)
    planted = jnp.where(in_first, chance < 8, chance == 0) | forced
    level_pick = jnp.where(forced, 2, jax.random.randint(level_key, (N_SECTION, L), 0, 3))
    amount = jnp.where(level_pick == 0, 0.7, jnp.where(level_pick == 1, 1.2, 3.0))
    amount = jnp.where(planted, amount, 0.0)
    return (noise_part + amount[..., None] * direction).astype(jnp.bfloat16)


def draw_kv_weight(key, part):
    direction, pattern = plant_signs(key)
    random_part = jax.random.truncated_normal(jax.random.fold_in(key, 21), -4.0, 4.0, (N_SECTION, D, 2 * KVH * HD), jnp.float32) * D ** (-0.5)
    columns = jnp.stack([pattern, jnp.zeros_like(pattern)], 0).reshape(-1)
    columns = jnp.tile(columns, KVH)
    return (random_part + plant_strength() * direction[:, None] * columns[None, :]).astype(jnp.bfloat16)


def draw_attn_flat(key, part):
    direction, pattern = plant_signs(key)
    query_width = QH * HD // N_MP
    whole_length = N_DP * SHARD
    random_part = jax.random.truncated_normal(jax.random.fold_in(key, 31), -4.0, 4.0, (N_SECTION, N_MP, whole_length), jnp.float32) * D ** (-0.5)
    planted_row = (direction[:, None] * jnp.tile(pattern, query_width // HD)[None, :]).reshape(-1) * plant_strength()
    planted_row = jnp.concatenate([planted_row, jnp.zeros((whole_length - D * query_width,), jnp.float32)])
    return (random_part + planted_row).astype(jnp.bfloat16)


def split_up(number_of, total, limit, lean):
    loads = [(1 << 20) // math.isqrt(standing ** lean) + 1 for standing in range(2, number_of + 1)]
    surplus, given = total - limit - (number_of - 1), [1] * (number_of - 1)
    while surplus > 0:
        movable = [i for i in range(number_of - 1) if given[i] < limit]
        pool, remaining = sum([loads[i] for i in movable]), surplus
        for i in movable:
            extra = min(limit - given[i], max(1, remaining * loads[i] // pool), surplus)
            given[i] = given[i] + extra
            surplus = surplus - extra
    return np.array([limit] + given)


def uneven(stream_key, number_of, total, reach, lean):
    if number_of == 2:
        one = jax.random.randint(stream_key, (), max(1, total - reach), min(reach, total - 1) + 1)
        return jnp.stack([one, total - one])
    lengths = jnp.asarray(split_up(number_of, total, reach, lean), jnp.int32)
    twos = (number_of - 1) // 2
    donor, sink = lengths[1:1 + 2 * twos:2], lengths[2:2 + 2 * twos:2]
    room = jnp.minimum(donor - 1, reach - sink)
    passed = jax.random.randint(jax.random.fold_in(stream_key, 1), (twos,), 0, 1 << 20) % (room + 1)
    lengths = lengths.at[1:1 + 2 * twos:2].set(donor - passed).at[2:2 + 2 * twos:2].set(sink + passed)
    return lengths[jax.random.permutation(jax.random.fold_in(stream_key, 2), number_of)]


def noise(own_key, dims, deviation, most, kind=jnp.bfloat16):
    result = deviation * jax.random.normal(own_key, dims, jnp.float32)
    return jnp.clip(result, min=-most, max=most).astype(kind)


def setup_inputs(seed: int = 0) -> dict:
    arg_keys = jax.random.split(jax.random.key(seed), 9)
    return {
        "hidden": draw_hidden(jax.random.fold_in(arg_keys[8], 71), 0),
        "norm_gain": jnp.clip(1.0 + 0.1 * jax.random.normal(arg_keys[1], (N_SECTION, D), jnp.float32), 0.5, 1.5),
        "kv_weight": draw_kv_weight(jax.random.fold_in(arg_keys[8], 71), 0),
        "attn_flat": draw_attn_flat(jax.random.fold_in(arg_keys[8], 71), 0),
        "final_gain": jnp.clip(1.0 + 0.1 * jax.random.normal(arg_keys[4], (D,), jnp.float32), 0.5, 1.5),
        "reward_head": noise(arg_keys[5], (D,), D ** -0.5, 0.09375, jnp.float32),
        "segment_ids": jax.vmap(lambda own: jnp.searchsorted(jnp.cumsum(uneven(own, R + 1, N_DP, MOST, 0)), jnp.arange(N_DP), side="right"))(jax.random.split(arg_keys[6], N_SECTION)).reshape((N_SECTION, N_DP)).astype(jnp.int32),
        "ranks": jax.random.randint(arg_keys[7], (R,), 0, 1000).astype(jnp.int32),
    }


EPS = 1e-05

def block_attention(query, keyval, seg, kv_local, group):
    length = query.shape[0]
    q_four = query.reshape(length, kv_local, group, HD).astype(jnp.float32)
    pieces = keyval.reshape(length, kv_local, 2, HD).astype(jnp.float32)
    keys = pieces[:, :, 0]
    values = pieces[:, :, 1]
    pos = jnp.arange(length, dtype=jnp.int32)
    blk = pos // BLK
    seg_tok = seg[blk]
    earlier = (blk[None, :] < blk[:, None]) & ((seg_tok[None, :] == 0) | (seg_tok[None, :] == seg_tok[:, None]))
    same = (blk[None, :] == blk[:, None]) & (pos[None, :] <= pos[:, None])
    visible = earlier | same
    scores = jnp.einsum('tjgd,cjd->jgtc', q_four, keys) * HD ** (-0.5)
    scores = jnp.where(visible[None, None], scores, -1e+30)
    peak = lax.optimization_barrier(jnp.max(scores, -1, keepdims=True))
    weights = jnp.where(visible[None, None], jnp.exp(scores - peak), 0.0)
    total = lax.optimization_barrier(jnp.sum(weights, -1))
    rounded = lax.optimization_barrier(weights.astype(jnp.bfloat16)).astype(jnp.float32)
    mixed = jnp.einsum('jgtc,cjd->jgtd', rounded, values) / total[..., None]
    return mixed.transpose(2, 0, 1, 3).reshape(length, kv_local * group * HD).astype(jnp.bfloat16)

def reference(hidden, norm_gain, kv_weight, attn_flat, final_gain, reward_head, segment_ids, ranks):
    kv_local = KVH // N_MP
    group = QH // KVH
    q_width = kv_local * group * HD
    kv_width = 2 * kv_local * HD
    outputs = []
    for phase in range(N_SECTION):
        state = hidden[phase].astype(jnp.float32)
        normed = (state * lax.rsqrt(lax.optimization_barrier(jnp.mean(state * state, -1, keepdims=True)) + EPS) * norm_gain[phase]).astype(jnp.bfloat16)
        keyval = jnp.dot(normed, kv_weight[phase], preferred_element_type=jnp.float32).astype(jnp.bfloat16)
        summed = jnp.zeros(state.shape, jnp.float32)
        for lane in range(N_MP):
            flat = attn_flat[phase, lane]
            w_query = flat[:D * q_width].reshape(D, q_width)
            w_out = flat[D * q_width:2 * D * q_width].reshape(q_width, D)
            query = jnp.dot(normed, w_query, preferred_element_type=jnp.float32).astype(jnp.bfloat16)
            mixed = block_attention(query, keyval[:, lane * kv_width:(lane + 1) * kv_width], segment_ids[phase], kv_local, group)
            term = jnp.dot(mixed, w_out, preferred_element_type=jnp.float32)
            summed = summed + lax.optimization_barrier(term.astype(jnp.bfloat16)).astype(jnp.float32)
        outputs.append((state + summed).astype(jnp.bfloat16))
    next_hidden = jnp.stack([jnp.zeros_like(outputs[0])] + outputs[:-1])
    final = outputs[-1].astype(jnp.float32)
    seg = segment_ids[N_SECTION - 1]
    ends = lax.optimization_barrier(jnp.sum((seg[None, :] <= jnp.arange(1, R + 1, dtype=jnp.int32)[:, None]).astype(jnp.int32), 1)) - 1
    rows = final[(ends + 1) * BLK - 1]
    rewards = lax.optimization_barrier(jnp.sum(rows * final_gain * reward_head, -1)) * lax.rsqrt(lax.optimization_barrier(jnp.mean(rows * rows, -1)) + EPS)
    pair_loss = jnp.where(ranks[:, None] < ranks[None, :], jax.nn.softplus(rewards[None, :] - rewards[:, None]), 0.0)
    return (next_hidden, rewards, pair_loss)
```

```python
import functools

import jax
import jax.numpy as jnp
from jax import lax
from jax.experimental import pallas as pl
from jax.experimental.pallas import tpu as pltpu
from jax.sharding import PartitionSpec as P

HD = 128
QH = 32
KVH = 8


EPS = 1e-05


def passed_along(block, axis, distance):
    devices = range(lax.axis_size(axis))
    route = [(i - distance, i) for i in devices if i - distance in devices]
    return lax.ppermute(block, axis, route)


def gathered_shards(hidden, norm_gain, kv_weight, attn_flat, final_gain, reward_head, segment_ids, ranks):
    state = hidden[0]
    tokens = state.shape[0]
    width = state.shape[1]
    seg_row = segment_ids[0]
    blocks = lax.axis_size("dp")
    block = lax.axis_index("dp")
    phases = lax.axis_size("section")
    phase_now = lax.axis_index("section")
    responses = ranks.shape[0]
    state_wide = state.astype(jnp.float32)
    normed = (
        state_wide
        * lax.rsqrt(jnp.mean(state_wide * state_wide, -1, keepdims=True) + EPS)
        * norm_gain[0]
    ).astype(jnp.bfloat16)
    keyval = jnp.dot(normed, kv_weight[0], preferred_element_type=jnp.float32).astype(jnp.bfloat16)
    kv_local = keyval.shape[1] // (2 * HD)
    group = QH // KVH
    q_width = kv_local * group * HD
    flat = lax.all_gather(attn_flat[0, 0], "dp", axis=0, tiled=True)
    w_query = flat[: width * q_width].reshape(width, q_width)
    w_out = flat[width * q_width : 2 * width * q_width].reshape(q_width, width)
    query = jnp.dot(normed, w_query, preferred_element_type=jnp.float32).astype(jnp.bfloat16)
    query = query.reshape(tokens, kv_local, group, HD)
    block_ids = jnp.arange(blocks, dtype=jnp.int32)
    own_seg = jnp.sum(jnp.where(block_ids == block, seg_row, 0))
    query_pos = block * tokens + jnp.arange(tokens, dtype=jnp.int32)
    piece = lax.all_gather(keyval, "dp", axis=0, tiled=True)
    peak = jnp.full((kv_local, group, tokens), -1e30, jnp.float32)
    count = piece.shape[0]
    key_pos = jnp.arange(count, dtype=jnp.int32)
    key_block = key_pos // tokens
    key_seg = jnp.sum(jnp.where(key_block[:, None] == block_ids[None, :], seg_row[None, :], 0), 1)
    parts = piece.reshape(count, kv_local, 2, HD)
    keys = parts[:, :, 0]
    values = parts[:, :, 1]
    earlier = (key_block < block) & (key_block >= 0) & ((key_seg == 0) | (key_seg == own_seg))
    same = (key_block == block)[None, :] & (key_pos[None, :] <= query_pos[:, None])
    visible = earlier[None, :] | same
    scores = jnp.einsum("tjgd,cjd->jgtc", query, keys, preferred_element_type=jnp.float32) * HD ** (
        -0.5
    )
    scores = jnp.where(visible[None, None], scores, -1e30)
    new_peak = jnp.maximum(peak, jnp.max(scores, -1))
    weights = jnp.where(visible[None, None], jnp.exp(scores - new_peak[..., None]), 0.0)
    total = jnp.sum(weights, -1)
    accum = jnp.einsum(
        "jgtc,cjd->jgtd", weights.astype(jnp.bfloat16), values, preferred_element_type=jnp.float32
    )
    peak, total, accum = (new_peak, total, accum)
    mixed = (
        (accum / total[..., None])
        .transpose(2, 0, 1, 3)
        .reshape(tokens, q_width)
        .astype(jnp.bfloat16)
    )
    partial_value = jnp.dot(mixed, w_out, preferred_element_type=jnp.float32)
    ends = (
        jnp.sum(
            (seg_row[None, :] <= jnp.arange(1, responses + 1, dtype=jnp.int32)[:, None]).astype(
                jnp.int32
            ),
            1,
        )
        - 1
    )
    at_end = (ends == block) & (phase_now == phases - 1)
    summed = lax.psum(partial_value.astype(jnp.bfloat16), "mp").astype(jnp.float32)
    updated = (state_wide + summed).astype(jnp.bfloat16)
    moved = passed_along(updated, "section", 1)
    last_row = updated[tokens - 1].astype(jnp.float32)
    squares = jnp.sum(last_row * last_row)
    product = jnp.sum(last_row * final_gain * reward_head)
    sums_sq, dots = lax.psum(
        (jnp.where(at_end, squares, 0.0), jnp.where(at_end, product, 0.0)), ("section", "dp")
    )
    rewards = dots * lax.rsqrt(sums_sq / width + EPS)
    pair_loss = jnp.where(
        ranks[:, None] < ranks[None, :], jax.nn.softplus(rewards[None, :] - rewards[:, None]), 0.0
    )
    return (moved[None], rewards, pair_loss)


BF = jnp.bfloat16
F32 = jnp.float32
HIDE = -1e30


def copy_to(src, dst, send, recv, **where):
    return pltpu.make_async_remote_copy(
        src_ref=src,
        dst_ref=dst,
        send_sem=send,
        recv_sem=recv,
        device_id=where,
        device_id_type=pl.DeviceIdType.MESH,
    )


def relay_kernel(
    phases,
    h_ref,
    gain_ref,
    kvw_hbm,
    flat_hbm,
    hide_ref,
    pick_ref,
    fg_ref,
    rh_ref,
    out_ref,
    stat_ref,
    kvw,
    flat,
    wq,
    wo,
    nrm,
    xq,
    kvs,
    kvr,
    qs,
    qo,
    qr,
    mx,
    mr,
    osend,
    oown,
    orecv,
    ysend,
    yown,
    yrecv,
    zsend,
    zrecv,
    ts,
    tr,
    us,
    fin,
    st,
    res,
    sres,
    load_sem,
    nz_s,
    nz_r,
    nm_s,
    nm_r,
    kv_s,
    kv_r,
    q_s,
    q_r,
    m_s,
    m_r,
    o_s,
    o_r,
    y_s,
    y_r,
    z_s,
    z_r,
    t_s,
    t_r,
    u_s,
    u_r,
    f_s,
    f_r,
    st_s,
    st_r,
    sr_s,
    sr_r,
):
    s = lax.axis_index("section")
    d = lax.axis_index("dp")
    m = lax.axis_index("mp")
    y = m // 2
    c = m % 2
    across = (m + 2) % 4
    beside = m + 1 - 2 * c
    load_kv = pltpu.make_async_copy(kvw_hbm.at[0], kvw, load_sem.at[0])
    load_flat = pltpu.make_async_copy(flat_hbm, flat, load_sem.at[1])
    load_kv.start()
    load_flat.start()

    barrier = pltpu.get_barrier_semaphore()
    place = d * 4 + m
    for k in range(1, 16):
        t = (place + k) % 16
        pl.semaphore_signal(
            barrier,
            inc=1,
            device_id={"dp": t // 4, "mp": t % 4},
            device_id_type=pl.DeviceIdType.MESH,
        )
    for k in range(1, phases):
        pl.semaphore_signal(
            barrier,
            inc=1,
            device_id={"section": (s + k) % phases},
            device_id_type=pl.DeviceIdType.MESH,
        )
    h = h_ref[...].astype(F32)
    scale = lax.rsqrt(jnp.mean(h * h, -1, keepdims=True) + EPS)
    nrm[...] = (h * scale * gain_ref[...]).astype(BF)
    pl.semaphore_wait(barrier, 15 + phases - 1)

    quarter = pl.ds(pl.multiple_of(m * 32, 32), 32)
    far_quarter = pl.ds(pl.multiple_of(across * 32, 32), 32)

    def hop_z(t):
        return copy_to(
            nrm.at[quarter, t * 2048 : (t + 1) * 2048],
            xq.at[d, quarter],
            nz_s.at[t],
            nz_r.at[d],
            dp=t,
        )

    def arrive_z(b):
        return copy_to(xq.at[b, quarter], xq.at[b, quarter], nz_s.at[0], nz_r.at[b], dp=b)

    def spread(b, k):
        rows = far_quarter if k == 2 else quarter
        return copy_to(
            xq.at[b, rows],
            xq.at[b, rows],
            nm_s.at[b, k],
            nm_r.at[b, k],
            mp=across if k == 0 else beside,
        )

    def kv_hop(t):
        return copy_to(kvs.at[t], kvr.at[d], kv_s.at[t], kv_r.at[d], dp=t)

    def kv_arrive(b):
        return copy_to(kvr.at[b], kvr.at[b], kv_s.at[0], kv_r.at[b], dp=b)

    for t in range(2):

        @pl.when(d != t)
        def _():
            hop_z(t).start()

        @pl.when(d == t)
        def _():
            xq[t] = nrm[:, t * 2048 : (t + 1) * 2048]

    load_kv.wait()
    for t in range(2):
        kvs[t] = jnp.dot(
            nrm[...], kvw[:, t * 256 : (t + 1) * 256], preferred_element_type=F32
        ).astype(BF)

        @pl.when(d != t)
        def _():
            kv_hop(t).start()

        @pl.when(d == t)
        def _():
            kvr[t] = kvs[t]

    load_flat.wait()

    def q_copy(b):
        return copy_to(qs.at[b], qr.at[b], q_s.at[b], q_r.at[b], dp=1 - d)

    def m_copy(b):
        return copy_to(mx.at[b], mr.at[b], m_s.at[b], m_r.at[b], dp=d + 2)

    def m_arrive(b):
        return copy_to(mr.at[b], mr.at[b], m_s.at[b], m_r.at[b], dp=d - 2)

    @pl.when(d < 2)
    def _():
        for b in range(4):

            @pl.loop(0, 8)
            def _(i):
                i = i + b * 8
                part = flat[0, :, pl.ds(pl.multiple_of(i * 65536, 65536), 65536)].astype(F32)
                wq[pl.ds(pl.multiple_of(i * 64, 64), 64), :] = part.reshape(64, 1024).astype(BF)

            @pl.when(d != b)
            def _():
                arrive_z(b).wait_recv()
                spread(b, 0).start()
                spread(b, 1).start()

        def forward(b):
            @pl.when(d != b)
            def _():
                spread(b, 0).wait_recv()
                spread(b, 2).start()

        def project(b):
            @pl.when(d != b)
            def _():
                spread(b, 1).wait_recv()
                spread(b, 2).wait_recv()

            mine = pl.ds(pl.multiple_of(d * 512, 512), 512)
            other = pl.ds(pl.multiple_of((1 - d) * 512, 512), 512)
            qs[b] = jnp.dot(xq[b], wq[:, other], preferred_element_type=F32).astype(BF)
            q_copy(b).start()
            qo[b] = jnp.dot(xq[b], wq[:, mine], preferred_element_type=F32)

        def attend(b):
            q_copy(b).wait_recv()

            @pl.when(d != b)
            def _():
                kv_arrive(b).wait_recv()

            q = (qo[b] + qr[b].astype(F32)).astype(BF)
            q = jnp.concatenate([q[:, j * HD : (j + 1) * HD] for j in range(4)], 0)
            scores = []
            for j in range(b + 1):
                score = (
                    lax.dot_general(
                        q, kvr[j, :, :HD], (((1,), (1,)), ((), ())), preferred_element_type=F32
                    )
                    * HD ** (-0.5)
                )
                if j < b:
                    score = score + hide_ref[b * 4 + j : b * 4 + j + 1, :]
                else:
                    row = lax.broadcasted_iota(jnp.int32, score.shape, 0) % 128
                    col = lax.broadcasted_iota(jnp.int32, score.shape, 1)
                    score = jnp.where(col <= row, score, HIDE)
                scores.append(score)
            peak = functools.reduce(jnp.maximum, [jnp.max(x, -1, keepdims=True) for x in scores])
            total = jnp.zeros_like(peak)
            mixed = jnp.zeros((512, HD), F32)
            for j in range(b + 1):
                weight = jnp.exp(scores[j] - peak)
                total = total + jnp.sum(weight, -1, keepdims=True)
                mixed = mixed + jnp.dot(
                    weight.astype(BF), kvr[j, :, HD:], preferred_element_type=F32
                )
            mixed = (mixed / total).astype(BF)
            for j in range(4):
                mx[b, :, j * HD : (j + 1) * HD] = mixed[j * 128 : (j + 1) * 128]
            m_copy(b).start()

        forward(0)
        for b in range(5):
            if b < 3:
                forward(b + 1)
            if b < 4:
                project(b)
            if b >= 1:
                attend(b - 1)

    def o_copy(b):
        return copy_to(osend.at[b], orecv.at[b], o_s.at[b], o_r.at[b], mp=beside)

    def y_copy(b):
        return copy_to(ysend.at[b], yrecv.at[b], y_s.at[b], y_r.at[b], mp=across)

    def z_copy(b):
        return copy_to(zsend.at[b], zrecv.at[b], z_s.at[b], z_r.at[b], dp=5 - d)

    def t_copy(b):
        return copy_to(ts.at[b], tr, t_s.at[b], t_r, dp=b)

    def t_arrive():
        return copy_to(tr, tr, t_s.at[0], t_r, dp=2)

    mine_out = pl.ds(pl.multiple_of((2 * c + y) * 1024, 1024), 1024)

    def finish(total):
        fresh = (h_ref[:, mine_out].astype(F32) + total).astype(BF)
        us[...] = fresh

    @pl.when(d >= 2)
    def _():
        @pl.loop(0, 32)
        def _(i):
            part = flat[0, :, pl.ds(pl.multiple_of(i * 65536, 65536), 65536)].astype(F32)
            wo[pl.ds(pl.multiple_of(i * 16, 16), 16), :] = part.reshape(16, 4096).astype(BF)

        def first(b):
            m_arrive(b).wait_recv()
            mine = pl.ds(pl.multiple_of(c * 2048, 2048), 2048)
            other = pl.ds(pl.multiple_of((1 - c) * 2048, 2048), 2048)
            osend[b] = jnp.dot(mr[b], wo[:, other], preferred_element_type=F32).astype(BF)
            o_copy(b).start()
            oown[b] = jnp.dot(mr[b], wo[:, mine], preferred_element_type=F32)

        def second(b):
            o_copy(b).wait_recv()
            mine = pl.ds(pl.multiple_of(y * 1024, 1024), 1024)
            other = pl.ds(pl.multiple_of((1 - y) * 1024, 1024), 1024)
            ysend[b] = (oown[b, :, other] + orecv[b, :, other].astype(F32)).astype(BF)
            y_copy(b).start()
            yown[b] = oown[b, :, mine] + orecv[b, :, mine].astype(F32)

        def third(b):
            y_copy(b).wait_recv()
            keeper = 3 if b == 3 else 2

            @pl.when(d != keeper)
            def _():
                zsend[b] = (yown[b] + yrecv[b].astype(F32)).astype(BF)
                z_copy(b).start()

            @pl.when(d == keeper)
            def _():
                yown[b] = yown[b] + yrecv[b].astype(F32)

        def fourth(b):
            keeper = 3 if b == 3 else 2

            @pl.when(d == keeper)
            def _():
                z_copy(b).wait_recv()
                total = yown[b] + zrecv[b].astype(F32)
                if b < 2:
                    ts[b] = total.astype(BF)
                    t_copy(b).start()
                else:
                    finish(total)

        for step in range(7):
            for part, stage in enumerate((first, second, third, fourth)):
                if 0 <= step - part < 4:
                    stage(step - part)

    @pl.when(d < 2)
    def _():
        t_arrive().wait_recv()
        finish(tr[...].astype(F32))

    def u_copy():
        return copy_to(us, fin.at[m], u_s, u_r, section=s + 1)

    def u_arrive():
        return copy_to(fin.at[m], fin.at[m], u_s, u_r, section=s - 1)

    def f_copy(k):
        which = across if k == 2 else m
        return copy_to(
            fin.at[which], fin.at[which], f_s.at[k], f_r.at[k], mp=across if k == 0 else beside
        )

    @pl.when(s < phases - 1)
    def _():
        u_copy().start()

    row = us[120:128, :].astype(F32)[7:8, :]
    squares = jnp.sum(row * row, keepdims=True)
    product = jnp.sum(row * fg_ref[:, mine_out] * rh_ref[:, mine_out], keepdims=True)
    half = lax.broadcasted_iota(jnp.int32, (8, 128), 0) < 4
    st[place] = jnp.where(half, squares, product)

    def st_copy(k):
        t = (place + k) % 16
        return pltpu.make_async_remote_copy(
            src_ref=st.at[place],
            dst_ref=st.at[place],
            send_sem=st_s.at[k - 1],
            recv_sem=st_r.at[k - 1],
            device_id={"dp": t // 4, "mp": t % 4},
            device_id_type=pl.DeviceIdType.MESH,
        )

    def st_arrive(k):
        t = (place + 16 - k) % 16
        return pltpu.make_async_remote_copy(
            src_ref=st.at[t],
            dst_ref=st.at[t],
            send_sem=st_s.at[k - 1],
            recv_sem=st_r.at[k - 1],
            device_id={"dp": t // 4, "mp": t % 4},
            device_id_type=pl.DeviceIdType.MESH,
        )

    def sr_copy(k):
        return copy_to(res, sres, sr_s.at[k - 1], sr_r, section=(s + k) % phases)

    @pl.when(s == phases - 1)
    def _():
        for k in range(1, 16):
            st_copy(k).start()

    @pl.when(s == 0)
    def _():
        out_ref[...] = jnp.zeros_like(out_ref)

    @pl.when(s > 0)
    def _():
        u_arrive().wait_recv()
        f_copy(0).start()
        f_copy(1).start()
        f_copy(0).wait_recv()
        f_copy(2).start()

    @pl.when(s == phases - 1)
    def _():
        for k in range(1, 16):
            st_arrive(k).wait_recv()
        for r in range(pick_ref.shape[0]):
            at_end = jnp.zeros((8, 128), F32)
            for b in range(4):
                block = st[4 * b] + st[4 * b + 1] + st[4 * b + 2] + st[4 * b + 3]
                at_end = at_end + jnp.where(pick_ref[r, b] > 0, block, 0.0)
            res[r] = at_end
        for k in range(1, phases):
            sr_copy(k).start()
        stat_ref[...] = res[...]

    @pl.when(s > 0)
    def _():
        f_copy(1).wait_recv()
        f_copy(2).wait_recv()
        for k in range(4):
            spot = 2 * (k % 2) + k // 2
            out_ref[:, spot * 1024 : (spot + 1) * 1024] = fin[k]
        for k in range(3):
            f_copy(k).wait_send()

    @pl.when(s < phases - 1)
    def _():
        sr_copy(1).wait_recv()
        stat_ref[...] = sres[...]
        u_copy().wait_send()

    @pl.when(s == phases - 1)
    def _():
        for k in range(1, 16):
            st_copy(k).wait_send()
        for k in range(1, phases):
            sr_copy(k).wait_send()

    for t in range(2):

        @pl.when(d != t)
        def _():
            hop_z(t).wait_send()
            kv_hop(t).wait_send()

    @pl.when(d < 2)
    def _():
        for b in range(4):

            @pl.when(d != b)
            def _():
                for k in range(3):
                    spread(b, k).wait_send()

            q_copy(b).wait_send()
            m_copy(b).wait_send()

    @pl.when(d >= 2)
    def _():
        for b in range(4):
            o_copy(b).wait_send()
            y_copy(b).wait_send()
            keeper = 3 if b == 3 else 2

            @pl.when(d != keeper)
            def _():
                z_copy(b).wait_send()

            if b < 2:

                @pl.when(d == keeper)
                def _():
                    t_copy(b).wait_send()


def kept_shards(hidden, norm_gain, kv_weight, attn_flat, final_gain, reward_head, segment_ids, ranks):
    width = hidden.shape[2]
    seg = segment_ids[0]
    phases = lax.axis_size("section")
    responses = ranks.shape[0]
    seen = (seg[None, :] == 0) | (seg[None, :] == seg[:, None])
    hide = jnp.broadcast_to(jnp.where(seen, 0.0, HIDE).reshape(16, 1), (16, 128)).astype(F32)
    level = jnp.arange(1, responses + 1, dtype=jnp.int32)
    ends = jnp.sum((seg[None, :] <= level[:, None]).astype(jnp.int32), 1) - 1
    pick = (ends[:, None] == jnp.arange(4, dtype=jnp.int32)[None, :]).astype(F32)
    pick = jnp.broadcast_to(pick[:, :, None, None], (responses, 4, 8, 128))
    vmem = pl.BlockSpec(memory_space=pltpu.VMEM)
    anywhere = pl.BlockSpec(memory_space=pl.ANY)
    dma = pltpu.SemaphoreType.DMA
    V = pltpu.VMEM
    moved, stats = pl.pallas_call(
        functools.partial(relay_kernel, phases),
        out_shape=(
            jax.ShapeDtypeStruct((128, 4096), BF),
            jax.ShapeDtypeStruct((responses, 8, 128), F32),
        ),
        in_specs=[vmem, vmem, anywhere, anywhere, vmem, vmem, vmem, vmem],
        out_specs=(vmem, vmem),
        scratch_shapes=[
            V((4096, 512), BF),
            V((1, 1, 2097152), BF),
            V((2048, 1024), BF),
            V((512, 4096), BF),
            V((128, 4096), BF),
            V((4, 128, 2048), BF),
            V((2, 128, 256), BF),
            V((4, 128, 256), BF),
            V((4, 128, 512), BF),
            V((4, 128, 512), F32),
            V((4, 128, 512), BF),
            V((4, 128, 512), BF),
            V((4, 128, 512), BF),
            V((4, 128, 2048), BF),
            V((4, 128, 2048), F32),
            V((4, 128, 2048), BF),
            V((4, 128, 1024), BF),
            V((4, 128, 1024), F32),
            V((4, 128, 1024), BF),
            V((4, 128, 1024), BF),
            V((4, 128, 1024), BF),
            V((2, 128, 1024), BF),
            V((128, 1024), BF),
            V((128, 1024), BF),
            V((4, 128, 1024), BF),
            V((16, 8, 128), F32),
            V((responses, 8, 128), F32),
            V((responses, 8, 128), F32),
            dma((2,)),
            dma((2,)),
            dma((4,)),
            dma((4, 3)),
            dma((4, 3)),
            dma((2,)),
            dma((4,)),
            dma((4,)),
            dma((4,)),
            dma((4,)),
            dma((4,)),
            dma((4,)),
            dma((4,)),
            dma((4,)),
            dma((4,)),
            dma((4,)),
            dma((4,)),
            dma((2,)),
            dma(()),
            dma(()),
            dma(()),
            dma((3,)),
            dma((3,)),
            dma((15,)),
            dma((15,)),
            dma((max(phases - 1, 1),)),
            dma(()),
        ],
        compiler_params=pltpu.CompilerParams(
            collective_id=0, has_side_effects=True, vmem_limit_bytes=60 << 20
        ),
    )(
        hidden[0],
        norm_gain,
        kv_weight,
        attn_flat,
        hide,
        pick,
        final_gain[None],
        reward_head[None],
    )
    rewards = stats[:, 4, 0] * lax.rsqrt(stats[:, 0, 0] / width + EPS)
    pair_loss = jnp.where(
        ranks[:, None] < ranks[None, :], jax.nn.softplus(rewards[None, :] - rewards[:, None]), 0.0
    )
    return (moved[None], rewards, pair_loss)


def shards(hidden, norm_gain, kv_weight, attn_flat, final_gain, reward_head, segment_ids, ranks):
    blocks = lax.axis_size("dp")
    lanes = lax.axis_size("mp")
    kv_local = kv_weight.shape[2] // (2 * HD)
    kept = (
        (blocks, lanes, kv_local) == (4, 4, 2)
        and hidden.shape[1:] == (128, 4096)
        and attn_flat.shape == (1, 1, 2097152)
    )
    args = (hidden, norm_gain, kv_weight, attn_flat, final_gain, reward_head, segment_ids, ranks)
    return (kept_shards if kept else gathered_shards)(*args)


def solution(mesh):
    placed = (
        P("section", "dp", None),
        P("section", None),
        P("section", None, "mp"),
        P("section", "mp", "dp"),
        P(),
        P(),
        P("section", None),
        P(),
    )
    return jax.shard_map(
        shards,
        mesh=mesh,
        in_specs=placed,
        out_specs=(P("section", "dp", None), P(), P()),
        check_vma=False,
    )
```

```python
import functools

import jax
import jax.numpy as jnp
from jax import lax
from jax.experimental import pallas as pl
from jax.experimental.pallas import tpu as pltpu
from jax.sharding import PartitionSpec as P

HD = 128
QH = 32
KVH = 8


EPS = 1e-05


def passed_along(block, axis, distance):
    devices = range(lax.axis_size(axis))
    route = [(i - distance, i) for i in devices if i - distance in devices]
    return lax.ppermute(block, axis, route)


def gathered_shards(hidden, norm_gain, kv_weight, attn_flat, final_gain, reward_head, segment_ids, ranks):
    state = hidden[0]
    tokens = state.shape[0]
    width = state.shape[1]
    seg_row = segment_ids[0]
    blocks = lax.axis_size("dp")
    block = lax.axis_index("dp")
    phases = lax.axis_size("section")
    phase_now = lax.axis_index("section")
    responses = ranks.shape[0]
    state_wide = state.astype(jnp.float32)
    normed = (
        state_wide
        * lax.rsqrt(jnp.mean(state_wide * state_wide, -1, keepdims=True) + EPS)
        * norm_gain[0]
    ).astype(jnp.bfloat16)
    keyval = jnp.dot(normed, kv_weight[0], preferred_element_type=jnp.float32).astype(jnp.bfloat16)
    kv_local = keyval.shape[1] // (2 * HD)
    group = QH // KVH
    q_width = kv_local * group * HD
    flat = lax.all_gather(attn_flat[0, 0], "dp", axis=0, tiled=True)
    w_query = flat[: width * q_width].reshape(width, q_width)
    w_out = flat[width * q_width : 2 * width * q_width].reshape(q_width, width)
    query = jnp.dot(normed, w_query, preferred_element_type=jnp.float32).astype(jnp.bfloat16)
    query = query.reshape(tokens, kv_local, group, HD)
    block_ids = jnp.arange(blocks, dtype=jnp.int32)
    own_seg = jnp.sum(jnp.where(block_ids == block, seg_row, 0))
    query_pos = block * tokens + jnp.arange(tokens, dtype=jnp.int32)
    piece = lax.all_gather(keyval, "dp", axis=0, tiled=True)
    peak = jnp.full((kv_local, group, tokens), -1e30, jnp.float32)
    count = piece.shape[0]
    key_pos = jnp.arange(count, dtype=jnp.int32)
    key_block = key_pos // tokens
    key_seg = jnp.sum(jnp.where(key_block[:, None] == block_ids[None, :], seg_row[None, :], 0), 1)
    parts = piece.reshape(count, kv_local, 2, HD)
    keys = parts[:, :, 0]
    values = parts[:, :, 1]
    earlier = (key_block < block) & (key_block >= 0) & ((key_seg == 0) | (key_seg == own_seg))
    same = (key_block == block)[None, :] & (key_pos[None, :] <= query_pos[:, None])
    visible = earlier[None, :] | same
    scores = jnp.einsum("tjgd,cjd->jgtc", query, keys, preferred_element_type=jnp.float32) * HD ** (
        -0.5
    )
    scores = jnp.where(visible[None, None], scores, -1e30)
    new_peak = jnp.maximum(peak, jnp.max(scores, -1))
    weights = jnp.where(visible[None, None], jnp.exp(scores - new_peak[..., None]), 0.0)
    total = jnp.sum(weights, -1)
    accum = jnp.einsum(
        "jgtc,cjd->jgtd", weights.astype(jnp.bfloat16), values, preferred_element_type=jnp.float32
    )
    peak, total, accum = (new_peak, total, accum)
    mixed = (
        (accum / total[..., None])
        .transpose(2, 0, 1, 3)
        .reshape(tokens, q_width)
        .astype(jnp.bfloat16)
    )
    partial_value = jnp.dot(mixed, w_out, preferred_element_type=jnp.float32)
    ends = (
        jnp.sum(
            (seg_row[None, :] <= jnp.arange(1, responses + 1, dtype=jnp.int32)[:, None]).astype(
                jnp.int32
            ),
            1,
        )
        - 1
    )
    at_end = (ends == block) & (phase_now == phases - 1)
    summed = lax.psum(partial_value.astype(jnp.bfloat16), "mp").astype(jnp.float32)
    updated = (state_wide + summed).astype(jnp.bfloat16)
    moved = passed_along(updated, "section", 1)
    last_row = updated[tokens - 1].astype(jnp.float32)
    squares = jnp.sum(last_row * last_row)
    product = jnp.sum(last_row * final_gain * reward_head)
    sums_sq, dots = lax.psum(
        (jnp.where(at_end, squares, 0.0), jnp.where(at_end, product, 0.0)), ("section", "dp")
    )
    rewards = dots * lax.rsqrt(sums_sq / width + EPS)
    pair_loss = jnp.where(
        ranks[:, None] < ranks[None, :], jax.nn.softplus(rewards[None, :] - rewards[:, None]), 0.0
    )
    return (moved[None], rewards, pair_loss)


BF = jnp.bfloat16
F32 = jnp.float32
HIDE = -1e30


def copy_to(src, dst, send, recv, **where):
    return pltpu.make_async_remote_copy(
        src_ref=src,
        dst_ref=dst,
        send_sem=send,
        recv_sem=recv,
        device_id=where,
        device_id_type=pl.DeviceIdType.MESH,
    )


def relay_kernel(
    phases,
    h_ref,
    gain_ref,
    kvw_hbm,
    flat_hbm,
    seg_ref,
    fg_ref,
    rh_ref,
    out_ref,
    stat_ref,
    kvw,
    flat,
    wq,
    wo,
    nrm,
    xq,
    kvs,
    kvr,
    qs,
    qo,
    qr,
    mx,
    mr,
    osend,
    oown,
    orecv,
    ysend,
    yown,
    yrecv,
    zsend,
    zrecv,
    ts,
    tr,
    us,
    fin,
    st,
    res,
    sres,
    load_sem,
    nz_s,
    nz_r,
    nm_s,
    nm_r,
    kv_s,
    kv_r,
    q_s,
    q_r,
    m_s,
    m_r,
    o_s,
    o_r,
    y_s,
    y_r,
    z_s,
    z_r,
    t_s,
    t_r,
    u_s,
    u_r,
    f_s,
    f_r,
    st_s,
    st_r,
    sr_s,
    sr_r,
):
    s = lax.axis_index("section")
    d = lax.axis_index("dp")
    m = lax.axis_index("mp")
    y = m // 2
    c = m % 2
    across = (m + 2) % 4
    beside = m + 1 - 2 * c
    load_kv = pltpu.make_async_copy(kvw_hbm.at[0], kvw, load_sem.at[0])
    load_flat = pltpu.make_async_copy(flat_hbm, flat, load_sem.at[1])
    load_kv.start()
    load_flat.start()

    barrier = pltpu.get_barrier_semaphore()
    place = d * 4 + m
    for k in range(1, 16):
        t = (place + k) % 16
        pl.semaphore_signal(
            barrier,
            inc=1,
            device_id={"dp": t // 4, "mp": t % 4},
            device_id_type=pl.DeviceIdType.MESH,
        )
    for k in range(1, phases):
        pl.semaphore_signal(
            barrier,
            inc=1,
            device_id={"section": (s + k) % phases},
            device_id_type=pl.DeviceIdType.MESH,
        )
    h = h_ref[...].astype(F32)
    scale = lax.rsqrt(jnp.mean(h * h, -1, keepdims=True) + EPS)
    nrm[...] = (h * scale * gain_ref[...]).astype(BF)
    pl.semaphore_wait(barrier, 15 + phases - 1)

    quarter = pl.ds(pl.multiple_of(m * 32, 32), 32)
    far_quarter = pl.ds(pl.multiple_of(across * 32, 32), 32)

    def hop_z(t):
        return copy_to(
            nrm.at[quarter, t * 2048 : (t + 1) * 2048],
            xq.at[d, quarter],
            nz_s.at[t],
            nz_r.at[d],
            dp=t,
        )

    def arrive_z(b):
        return copy_to(xq.at[b, quarter], xq.at[b, quarter], nz_s.at[0], nz_r.at[b], dp=b)

    def spread(b, k):
        rows = far_quarter if k == 2 else quarter
        return copy_to(
            xq.at[b, rows],
            xq.at[b, rows],
            nm_s.at[b, k],
            nm_r.at[b, k],
            mp=across if k == 0 else beside,
        )

    def kv_hop(t):
        return copy_to(kvs.at[t], kvr.at[d], kv_s.at[t], kv_r.at[d], dp=t)

    def kv_arrive(b):
        return copy_to(kvr.at[b], kvr.at[b], kv_s.at[0], kv_r.at[b], dp=b)

    for t in range(2):

        @pl.when(d != t)
        def _():
            hop_z(t).start()

        @pl.when(d == t)
        def _():
            xq[t] = nrm[:, t * 2048 : (t + 1) * 2048]

    load_kv.wait()
    for t in range(2):
        kvs[t] = jnp.dot(
            nrm[...], kvw[:, t * 256 : (t + 1) * 256], preferred_element_type=F32
        ).astype(BF)

        @pl.when(d != t)
        def _():
            kv_hop(t).start()

        @pl.when(d == t)
        def _():
            kvr[t] = kvs[t]

    load_flat.wait()

    def q_copy(b):
        return copy_to(qs.at[b], qr.at[b], q_s.at[b], q_r.at[b], dp=1 - d)

    def m_copy(b):
        return copy_to(mx.at[b], mr.at[b], m_s.at[b], m_r.at[b], dp=d + 2)

    def m_arrive(b):
        return copy_to(mr.at[b], mr.at[b], m_s.at[b], m_r.at[b], dp=d - 2)

    def piece(g, stage):
        if g % 2:
            stage(g)
        else:

            @pl.when(s < phases - 1)
            def _():
                stage(g)

    @pl.when(d < 2)
    def _():
        for b in range(4):

            @pl.loop(0, 8)
            def _(i):
                i = i + b * 8
                part = flat[0, :, pl.ds(pl.multiple_of(i * 65536, 65536), 65536)].astype(F32)
                wq[pl.ds(pl.multiple_of(i * 64, 64), 64), :] = part.reshape(64, 1024).astype(BF)

            @pl.when(d != b)
            def _():
                arrive_z(b).wait_recv()
                spread(b, 0).start()
                spread(b, 1).start()

        def forward(b):
            @pl.when(d != b)
            def _():
                spread(b, 0).wait_recv()
                spread(b, 2).start()

        def project(b):
            @pl.when(d != b)
            def _():
                spread(b, 1).wait_recv()
                spread(b, 2).wait_recv()

            mine = pl.ds(pl.multiple_of(d * 512, 512), 512)
            other = pl.ds(pl.multiple_of((1 - d) * 512, 512), 512)
            qs[b] = jnp.dot(xq[b], wq[:, other], preferred_element_type=F32).astype(BF)
            q_copy(b).start()
            qo[b] = jnp.dot(xq[b], wq[:, mine], preferred_element_type=F32)

        def ready(b):
            q_copy(b).wait_recv()

            @pl.when(d != b)
            def _():
                kv_arrive(b).wait_recv()

        def attend(g):
            b, half = g // 2, g % 2
            rows = slice(half * 64, half * 64 + 64)
            q = (qo[b, rows] + qr[b, rows].astype(F32)).astype(BF)
            q = jnp.concatenate([q[:, j * HD : (j + 1) * HD] for j in range(4)], 0)
            scores = []
            for j in range(b + 1):
                score = (
                    lax.dot_general(
                        q, kvr[j, :, :HD], (((1,), (1,)), ((), ())), preferred_element_type=F32
                    )
                    * HD ** (-0.5)
                )
                if j < b:
                    seen = (seg_ref[0, j] == 0) | (seg_ref[0, j] == seg_ref[0, b])
                    score = score + jnp.where(seen, 0.0, HIDE)
                else:
                    row = lax.broadcasted_iota(jnp.int32, score.shape, 0) % 64 + half * 64
                    col = lax.broadcasted_iota(jnp.int32, score.shape, 1)
                    score = jnp.where(col <= row, score, HIDE)
                scores.append(score)
            peak = functools.reduce(jnp.maximum, [jnp.max(x, -1, keepdims=True) for x in scores])
            total = jnp.zeros_like(peak)
            mixed = jnp.zeros((256, HD), F32)
            for j in range(b + 1):
                weight = jnp.exp(scores[j] - peak)
                total = total + jnp.sum(weight, -1, keepdims=True)
                mixed = mixed + jnp.dot(
                    weight.astype(BF), kvr[j, :, HD:], preferred_element_type=F32
                )
            mixed = (mixed / total).astype(BF)
            for j in range(4):
                mx[g, :, j * HD : (j + 1) * HD] = mixed[j * 64 : (j + 1) * 64]
            m_copy(g).start()

        forward(0)
        for b in range(5):
            if b < 3:
                forward(b + 1)
            if b < 4:
                project(b)
            if b >= 1:
                ready(b - 1)
                piece(2 * b - 2, attend)
                piece(2 * b - 1, attend)

    def o_copy(b):
        return copy_to(osend.at[b], orecv.at[b], o_s.at[b], o_r.at[b], mp=beside)

    def y_copy(b):
        return copy_to(ysend.at[b], yrecv.at[b], y_s.at[b], y_r.at[b], mp=across)

    def z_copy(b):
        return copy_to(zsend.at[b], zrecv.at[b], z_s.at[b], z_r.at[b], dp=5 - d)

    def t_copy(b):
        return copy_to(ts.at[b], tr.at[b % 2], t_s.at[b], t_r.at[b % 2], dp=b // 2)

    def t_arrive(p):
        return copy_to(tr.at[p], tr.at[p], t_s.at[0], t_r.at[p], dp=2)

    mine_out = pl.ds(pl.multiple_of((2 * c + y) * 1024, 1024), 1024)

    def u_copy(p):
        return copy_to(us.at[p], fin.at[p, m], u_s.at[p], u_r.at[p], section=s + 1)

    def u_arrive(p):
        return copy_to(fin.at[p, m], fin.at[p, m], u_s.at[p], u_r.at[p], section=s - 1)

    def f_copy(p, k):
        which = across if k == 2 else m
        return copy_to(
            fin.at[p, which],
            fin.at[p, which],
            f_s.at[p, k],
            f_r.at[p, k],
            mp=across if k == 0 else beside,
        )

    def finish(p, total):
        old = h_ref[p * 64 : p * 64 + 64, mine_out].astype(F32)
        us[p] = (old + total).astype(BF)

        @pl.when(s < phases - 1)
        def _():
            u_copy(p).start()

    @pl.when(d >= 2)
    def _():
        @pl.loop(0, 32)
        def _(i):
            part = flat[0, :, pl.ds(pl.multiple_of(i * 65536, 65536), 65536)].astype(F32)
            wo[pl.ds(pl.multiple_of(i * 16, 16), 16), :] = part.reshape(16, 4096).astype(BF)

        def first(b):
            m_arrive(b).wait_recv()
            mine = pl.ds(pl.multiple_of(c * 2048, 2048), 2048)
            other = pl.ds(pl.multiple_of((1 - c) * 2048, 2048), 2048)
            osend[b] = jnp.dot(mr[b], wo[:, other], preferred_element_type=F32).astype(BF)
            o_copy(b).start()
            oown[b] = jnp.dot(mr[b], wo[:, mine], preferred_element_type=F32)

        def second(b):
            o_copy(b).wait_recv()
            mine = pl.ds(pl.multiple_of(y * 1024, 1024), 1024)
            other = pl.ds(pl.multiple_of((1 - y) * 1024, 1024), 1024)
            ysend[b] = (oown[b, :, other] + orecv[b, :, other].astype(F32)).astype(BF)
            y_copy(b).start()
            yown[b] = oown[b, :, mine] + orecv[b, :, mine].astype(F32)

        def third(b):
            y_copy(b).wait_recv()
            keeper = 3 if b >= 6 else 2

            @pl.when(d != keeper)
            def _():
                zsend[b] = (yown[b] + yrecv[b].astype(F32)).astype(BF)
                z_copy(b).start()

            @pl.when(d == keeper)
            def _():
                yown[b] = yown[b] + yrecv[b].astype(F32)

        def fourth(b):
            keeper = 3 if b >= 6 else 2

            @pl.when(d == keeper)
            def _():
                z_copy(b).wait_recv()
                total = yown[b] + zrecv[b].astype(F32)
                if b < 4:
                    ts[b] = total.astype(BF)
                    t_copy(b).start()
                else:
                    finish(b % 2, total)

        for step in range(11):
            for part, stage in enumerate((first, second, third, fourth)):
                if 0 <= step - part < 8:
                    piece(step - part, stage)

    @pl.when(d < 2)
    def _():
        def close(p):
            t_arrive(p).wait_recv()
            finish(p, tr[p].astype(F32))

        piece(0, close)
        piece(1, close)

    row = us[1, 48:64, :].astype(F32)[15:16, :]
    squares = jnp.sum(row * row, keepdims=True)
    product = jnp.sum(row * fg_ref[:, mine_out] * rh_ref[:, mine_out], keepdims=True)
    half = lax.broadcasted_iota(jnp.int32, (8, 128), 0) < 4
    st[place] = jnp.where(half, squares, product)

    def st_copy(k):
        t = (place + k) % 16
        return pltpu.make_async_remote_copy(
            src_ref=st.at[place],
            dst_ref=st.at[place],
            send_sem=st_s.at[k - 1],
            recv_sem=st_r.at[k - 1],
            device_id={"dp": t // 4, "mp": t % 4},
            device_id_type=pl.DeviceIdType.MESH,
        )

    def st_arrive(k):
        t = (place + 16 - k) % 16
        return pltpu.make_async_remote_copy(
            src_ref=st.at[t],
            dst_ref=st.at[t],
            send_sem=st_s.at[k - 1],
            recv_sem=st_r.at[k - 1],
            device_id={"dp": t // 4, "mp": t % 4},
            device_id_type=pl.DeviceIdType.MESH,
        )

    def sr_copy(k):
        return copy_to(res, sres, sr_s.at[k - 1], sr_r, section=(s + k) % phases)

    @pl.when(s == phases - 1)
    def _():
        for k in range(1, 16):
            st_copy(k).start()

    @pl.when(s == 0)
    def _():
        out_ref[...] = jnp.zeros_like(out_ref)

    @pl.when(s > 0)
    def _():
        for p in range(2):
            u_arrive(p).wait_recv()
            f_copy(p, 0).start()
            f_copy(p, 1).start()
        for p in range(2):
            f_copy(p, 0).wait_recv()
            f_copy(p, 2).start()

    @pl.when(s == phases - 1)
    def _():
        for k in range(1, 16):
            st_arrive(k).wait_recv()
        for r in range(res.shape[0]):
            end = -1
            for b in range(4):
                end = end + jnp.where(seg_ref[0, b] <= r + 1, 1, 0)
            at_end = jnp.zeros((8, 128), F32)
            for b in range(4):
                block = st[4 * b] + st[4 * b + 1] + st[4 * b + 2] + st[4 * b + 3]
                at_end = at_end + block * jnp.where(end == b, 1.0, 0.0)
            res[r] = at_end
        for k in range(1, phases):
            sr_copy(k).start()
        stat_ref[...] = res[...]

    @pl.when(s > 0)
    def _():
        for p in range(2):
            f_copy(p, 1).wait_recv()
            f_copy(p, 2).wait_recv()
            for k in range(4):
                out_ref[2 * (k % 2) + k // 2, p * 64 : p * 64 + 64] = fin[p, k]
        for p in range(2):
            for k in range(3):
                f_copy(p, k).wait_send()

    @pl.when(s < phases - 1)
    def _():
        sr_copy(1).wait_recv()
        stat_ref[...] = sres[...]
        for p in range(2):
            u_copy(p).wait_send()

    @pl.when(s == phases - 1)
    def _():
        for k in range(1, 16):
            st_copy(k).wait_send()
        for k in range(1, phases):
            sr_copy(k).wait_send()

    for t in range(2):

        @pl.when(d != t)
        def _():
            hop_z(t).wait_send()
            kv_hop(t).wait_send()

    @pl.when(d < 2)
    def _():
        for b in range(4):

            @pl.when(d != b)
            def _():
                for k in range(3):
                    spread(b, k).wait_send()

            q_copy(b).wait_send()
        for g in range(8):
            piece(g, lambda g: m_copy(g).wait_send())

    @pl.when(d >= 2)
    def _():
        def sent(g):
            o_copy(g).wait_send()
            y_copy(g).wait_send()
            keeper = 3 if g >= 6 else 2

            @pl.when(d != keeper)
            def _():
                z_copy(g).wait_send()

            if g < 4:

                @pl.when(d == keeper)
                def _():
                    t_copy(g).wait_send()

        for g in range(8):
            piece(g, sent)


def kept_shards(hidden, norm_gain, kv_weight, attn_flat, final_gain, reward_head, segment_ids, ranks):
    width = hidden.shape[2]
    phases = lax.axis_size("section")
    responses = ranks.shape[0]
    vmem = pl.BlockSpec(memory_space=pltpu.VMEM)
    anywhere = pl.BlockSpec(memory_space=pl.ANY)
    dma = pltpu.SemaphoreType.DMA
    V = pltpu.VMEM
    moved, stats = pl.pallas_call(
        functools.partial(relay_kernel, phases),
        out_shape=(
            jax.ShapeDtypeStruct((4, 128, 1024), BF),
            jax.ShapeDtypeStruct((responses, 8, 128), F32),
        ),
        in_specs=[
            vmem,
            vmem,
            anywhere,
            anywhere,
            pl.BlockSpec(memory_space=pltpu.SMEM),
            vmem,
            vmem,
        ],
        out_specs=(vmem, vmem),
        scratch_shapes=[
            V((4096, 512), BF),
            V((1, 1, 2097152), BF),
            V((2048, 1024), BF),
            V((512, 4096), BF),
            V((128, 4096), BF),
            V((4, 128, 2048), BF),
            V((2, 128, 256), BF),
            V((4, 128, 256), BF),
            V((4, 128, 512), BF),
            V((4, 128, 512), F32),
            V((4, 128, 512), BF),
            V((8, 64, 512), BF),
            V((8, 64, 512), BF),
            V((8, 64, 2048), BF),
            V((8, 64, 2048), F32),
            V((8, 64, 2048), BF),
            V((8, 64, 1024), BF),
            V((8, 64, 1024), F32),
            V((8, 64, 1024), BF),
            V((8, 64, 1024), BF),
            V((8, 64, 1024), BF),
            V((4, 64, 1024), BF),
            V((2, 64, 1024), BF),
            V((2, 64, 1024), BF),
            V((2, 4, 64, 1024), BF),
            V((16, 8, 128), F32),
            V((responses, 8, 128), F32),
            V((responses, 8, 128), F32),
            dma((2,)),
            dma((2,)),
            dma((4,)),
            dma((4, 3)),
            dma((4, 3)),
            dma((2,)),
            dma((4,)),
            dma((4,)),
            dma((4,)),
            dma((8,)),
            dma((8,)),
            dma((8,)),
            dma((8,)),
            dma((8,)),
            dma((8,)),
            dma((8,)),
            dma((8,)),
            dma((4,)),
            dma((2,)),
            dma((2,)),
            dma((2,)),
            dma((2, 3)),
            dma((2, 3)),
            dma((15,)),
            dma((15,)),
            dma((max(phases - 1, 1),)),
            dma(()),
        ],
        compiler_params=pltpu.CompilerParams(
            collective_id=0, has_side_effects=True, vmem_limit_bytes=60 << 20
        ),
    )(
        hidden[0],
        norm_gain,
        kv_weight,
        attn_flat,
        segment_ids,
        final_gain[None],
        reward_head[None],
    )
    rewards = stats[:, 4, 0] * lax.rsqrt(stats[:, 0, 0] / width + EPS)
    pair_loss = jnp.where(
        ranks[:, None] < ranks[None, :], jax.nn.softplus(rewards[None, :] - rewards[:, None]), 0.0
    )
    moved = moved.transpose(1, 0, 2).reshape(1, 128, width)
    return (moved, rewards, pair_loss)


def shards(hidden, norm_gain, kv_weight, attn_flat, final_gain, reward_head, segment_ids, ranks):
    blocks = lax.axis_size("dp")
    lanes = lax.axis_size("mp")
    kv_local = kv_weight.shape[2] // (2 * HD)
    kept = (
        (blocks, lanes, kv_local) == (4, 4, 2)
        and hidden.shape[1:] == (128, 4096)
        and attn_flat.shape == (1, 1, 2097152)
    )
    args = (hidden, norm_gain, kv_weight, attn_flat, final_gain, reward_head, segment_ids, ranks)
    return (kept_shards if kept else gathered_shards)(*args)


def solution(mesh):
    placed = (
        P("section", "dp", None),
        P("section", None),
        P("section", None, "mp"),
        P("section", "mp", "dp"),
        P(),
        P(),
        P("section", None),
        P(),
    )
    return jax.shard_map(
        shards,
        mesh=mesh,
        in_specs=placed,
        out_specs=(P("section", "dp", None), P(), P()),
        check_vma=False,
    )
```

```python
import functools

import jax
import jax.numpy as jnp
from jax import lax
from jax.experimental import pallas as pl
from jax.experimental.pallas import tpu as pltpu
from jax.sharding import PartitionSpec as P

HD = 128
QH = 32
KVH = 8


EPS = 1e-05


def passed_along(block, axis, distance):
    devices = range(lax.axis_size(axis))
    route = [(i - distance, i) for i in devices if i - distance in devices]
    return lax.ppermute(block, axis, route)


def gathered_shards(hidden, norm_gain, kv_weight, attn_flat, final_gain, reward_head, segment_ids, ranks):
    state = hidden[0]
    tokens = state.shape[0]
    width = state.shape[1]
    seg_row = segment_ids[0]
    blocks = lax.axis_size("dp")
    block = lax.axis_index("dp")
    phases = lax.axis_size("section")
    phase_now = lax.axis_index("section")
    responses = ranks.shape[0]
    state_wide = state.astype(jnp.float32)
    normed = (
        state_wide
        * lax.rsqrt(jnp.mean(state_wide * state_wide, -1, keepdims=True) + EPS)
        * norm_gain[0]
    ).astype(jnp.bfloat16)
    keyval = jnp.dot(normed, kv_weight[0], preferred_element_type=jnp.float32).astype(jnp.bfloat16)
    kv_local = keyval.shape[1] // (2 * HD)
    group = QH // KVH
    q_width = kv_local * group * HD
    flat = lax.all_gather(attn_flat[0, 0], "dp", axis=0, tiled=True)
    w_query = flat[: width * q_width].reshape(width, q_width)
    w_out = flat[width * q_width : 2 * width * q_width].reshape(q_width, width)
    query = jnp.dot(normed, w_query, preferred_element_type=jnp.float32).astype(jnp.bfloat16)
    query = query.reshape(tokens, kv_local, group, HD)
    block_ids = jnp.arange(blocks, dtype=jnp.int32)
    own_seg = jnp.sum(jnp.where(block_ids == block, seg_row, 0))
    query_pos = block * tokens + jnp.arange(tokens, dtype=jnp.int32)
    piece = lax.all_gather(keyval, "dp", axis=0, tiled=True)
    peak = jnp.full((kv_local, group, tokens), -1e30, jnp.float32)
    count = piece.shape[0]
    key_pos = jnp.arange(count, dtype=jnp.int32)
    key_block = key_pos // tokens
    key_seg = jnp.sum(jnp.where(key_block[:, None] == block_ids[None, :], seg_row[None, :], 0), 1)
    parts = piece.reshape(count, kv_local, 2, HD)
    keys = parts[:, :, 0]
    values = parts[:, :, 1]
    earlier = (key_block < block) & (key_block >= 0) & ((key_seg == 0) | (key_seg == own_seg))
    same = (key_block == block)[None, :] & (key_pos[None, :] <= query_pos[:, None])
    visible = earlier[None, :] | same
    scores = jnp.einsum("tjgd,cjd->jgtc", query, keys, preferred_element_type=jnp.float32) * HD ** (
        -0.5
    )
    scores = jnp.where(visible[None, None], scores, -1e30)
    new_peak = jnp.maximum(peak, jnp.max(scores, -1))
    weights = jnp.where(visible[None, None], jnp.exp(scores - new_peak[..., None]), 0.0)
    total = jnp.sum(weights, -1)
    accum = jnp.einsum(
        "jgtc,cjd->jgtd", weights.astype(jnp.bfloat16), values, preferred_element_type=jnp.float32
    )
    peak, total, accum = (new_peak, total, accum)
    mixed = (
        (accum / total[..., None])
        .transpose(2, 0, 1, 3)
        .reshape(tokens, q_width)
        .astype(jnp.bfloat16)
    )
    partial_value = jnp.dot(mixed, w_out, preferred_element_type=jnp.float32)
    ends = (
        jnp.sum(
            (seg_row[None, :] <= jnp.arange(1, responses + 1, dtype=jnp.int32)[:, None]).astype(
                jnp.int32
            ),
            1,
        )
        - 1
    )
    at_end = (ends == block) & (phase_now == phases - 1)
    summed = lax.psum(partial_value.astype(jnp.bfloat16), "mp").astype(jnp.float32)
    updated = (state_wide + summed).astype(jnp.bfloat16)
    moved = passed_along(updated, "section", 1)
    last_row = updated[tokens - 1].astype(jnp.float32)
    squares = jnp.sum(last_row * last_row)
    product = jnp.sum(last_row * final_gain * reward_head)
    sums_sq, dots = lax.psum(
        (jnp.where(at_end, squares, 0.0), jnp.where(at_end, product, 0.0)), ("section", "dp")
    )
    rewards = dots * lax.rsqrt(sums_sq / width + EPS)
    pair_loss = jnp.where(
        ranks[:, None] < ranks[None, :], jax.nn.softplus(rewards[None, :] - rewards[:, None]), 0.0
    )
    return (moved[None], rewards, pair_loss)


BF = jnp.bfloat16
F32 = jnp.float32
HIDE = -1e30


def copy_to(src, dst, send, recv, **where):
    return pltpu.make_async_remote_copy(
        src_ref=src,
        dst_ref=dst,
        send_sem=send,
        recv_sem=recv,
        device_id=where,
        device_id_type=pl.DeviceIdType.MESH,
    )


def relay_kernel(
    phases,
    h_ref,
    gain_ref,
    kvw_hbm,
    flat_hbm,
    seg_ref,
    fg_ref,
    rh_ref,
    out_ref,
    stat_ref,
    kvw,
    flat,
    wq,
    wo,
    nrm,
    xq,
    kvs,
    kvr,
    qs,
    qo,
    qr,
    mx,
    mr,
    osend,
    oown,
    orecv,
    ysend,
    yown,
    yrecv,
    zsend,
    zrecv,
    ts,
    tr,
    us,
    fin,
    st,
    res,
    sres,
    load_sem,
    nz_s,
    nz_r,
    nm_s,
    nm_r,
    kv_s,
    kv_r,
    q_s,
    q_r,
    m_s,
    m_r,
    o_s,
    o_r,
    y_s,
    y_r,
    z_s,
    z_r,
    t_s,
    t_r,
    u_s,
    u_r,
    f_s,
    f_r,
    st_s,
    st_r,
    sr_s,
    sr_r,
):
    s = lax.axis_index("section")
    d = lax.axis_index("dp")
    m = lax.axis_index("mp")
    y = m // 2
    c = m % 2
    across = (m + 2) % 4
    beside = m + 1 - 2 * c
    load_kv = pltpu.make_async_copy(kvw_hbm.at[0], kvw, load_sem.at[0])
    load_flat = pltpu.make_async_copy(flat_hbm, flat, load_sem.at[1])
    load_kv.start()
    load_flat.start()

    barrier = pltpu.get_barrier_semaphore()
    place = d * 4 + m
    for k in range(1, 16):
        t = (place + k) % 16
        pl.semaphore_signal(
            barrier,
            inc=1,
            device_id={"dp": t // 4, "mp": t % 4},
            device_id_type=pl.DeviceIdType.MESH,
        )
    for k in range(1, phases):
        pl.semaphore_signal(
            barrier,
            inc=1,
            device_id={"section": (s + k) % phases},
            device_id_type=pl.DeviceIdType.MESH,
        )
    h = h_ref[...].astype(F32)
    scale = lax.rsqrt(jnp.mean(h * h, -1, keepdims=True) + EPS)
    nrm[...] = (h * scale * gain_ref[...]).astype(BF)
    pl.semaphore_wait(barrier, 15 + phases - 1)

    quarter = pl.ds(pl.multiple_of(m * 32, 32), 32)
    far_quarter = pl.ds(pl.multiple_of(across * 32, 32), 32)

    def hop_z(t):
        return copy_to(
            nrm.at[quarter, t * 2048 : (t + 1) * 2048],
            xq.at[d, quarter],
            nz_s.at[t],
            nz_r.at[d],
            dp=t,
        )

    def arrive_z(b):
        return copy_to(xq.at[b, quarter], xq.at[b, quarter], nz_s.at[0], nz_r.at[b], dp=b)

    def spread(b, k):
        rows = far_quarter if k == 2 else quarter
        return copy_to(
            xq.at[b, rows],
            xq.at[b, rows],
            nm_s.at[b, k],
            nm_r.at[b, k],
            mp=across if k == 0 else beside,
        )

    def kv_hop(t):
        return copy_to(kvs.at[t], kvr.at[d], kv_s.at[t], kv_r.at[d], dp=t)

    def kv_arrive(b):
        return copy_to(kvr.at[b], kvr.at[b], kv_s.at[0], kv_r.at[b], dp=b)

    for t in range(2):

        @pl.when(d != t)
        def _():
            hop_z(t).start()

        @pl.when(d == t)
        def _():
            xq[t] = nrm[:, t * 2048 : (t + 1) * 2048]

    load_kv.wait()
    for t in range(2):
        kvs[t] = jnp.dot(
            nrm[...], kvw[:, t * 256 : (t + 1) * 256], preferred_element_type=F32
        ).astype(BF)

        @pl.when(d != t)
        def _():
            kv_hop(t).start()

        @pl.when(d == t)
        def _():
            kvr[t] = kvs[t]

    load_flat.wait()

    def q_copy(b):
        return copy_to(qs.at[b], qr.at[b], q_s.at[b], q_r.at[b], dp=1 - d)

    def m_copy(b):
        return copy_to(mx.at[b], mr.at[b], m_s.at[b], m_r.at[b], dp=d + 2)

    def m_arrive(b):
        return copy_to(mr.at[b], mr.at[b], m_s.at[b], m_r.at[b], dp=d - 2)

    def piece(g, stage):
        if g % 2:
            stage(g)
        else:

            @pl.when(s < phases - 1)
            def _():
                stage(g)

    @pl.when(d < 2)
    def _():
        def reshape(b):
            @pl.loop(0, 8)
            def _(i):
                i = i + b * 8
                part = flat[0, :, pl.ds(pl.multiple_of(i * 65536, 65536), 65536)].astype(F32)
                wq[pl.ds(pl.multiple_of(i * 64, 64), 64), :] = part.reshape(64, 1024).astype(BF)

        def receive(b):
            @pl.when(d != b)
            def _():
                arrive_z(b).wait_recv()
                spread(b, 0).start()
                spread(b, 1).start()

        def forward(b):
            @pl.when(d != b)
            def _():
                spread(b, 0).wait_recv()
                spread(b, 2).start()

        def project(b):
            @pl.when(d != b)
            def _():
                spread(b, 1).wait_recv()
                spread(b, 2).wait_recv()

            mine = pl.ds(pl.multiple_of(d * 512, 512), 512)
            other = pl.ds(pl.multiple_of((1 - d) * 512, 512), 512)
            qs[b] = jnp.dot(xq[b], wq[:, other], preferred_element_type=F32).astype(BF)
            q_copy(b).start()
            qo[b] = jnp.dot(xq[b], wq[:, mine], preferred_element_type=F32)

        def ready(b):
            q_copy(b).wait_recv()

            @pl.when(d != b)
            def _():
                kv_arrive(b).wait_recv()

        def attend(g):
            b, half = g // 2, g % 2
            rows = slice(half * 64, half * 64 + 64)
            q = (qo[b, rows] + qr[b, rows].astype(F32)).astype(BF)
            q = jnp.concatenate([q[:, j * HD : (j + 1) * HD] for j in range(4)], 0)
            scores = []
            for j in range(b + 1):
                score = (
                    lax.dot_general(
                        q, kvr[j, :, :HD], (((1,), (1,)), ((), ())), preferred_element_type=F32
                    )
                    * HD ** (-0.5)
                )
                if j < b:
                    seen = (seg_ref[0, j] == 0) | (seg_ref[0, j] == seg_ref[0, b])
                    score = score + jnp.where(seen, 0.0, HIDE)
                else:
                    row = lax.broadcasted_iota(jnp.int32, score.shape, 0) % 64 + half * 64
                    col = lax.broadcasted_iota(jnp.int32, score.shape, 1)
                    score = jnp.where(col <= row, score, HIDE)
                scores.append(score)
            peak = functools.reduce(jnp.maximum, [jnp.max(x, -1, keepdims=True) for x in scores])
            total = jnp.zeros_like(peak)
            mixed = jnp.zeros((256, HD), F32)
            for j in range(b + 1):
                weight = jnp.exp(scores[j] - peak)
                total = total + jnp.sum(weight, -1, keepdims=True)
                mixed = mixed + jnp.dot(
                    weight.astype(BF), kvr[j, :, HD:], preferred_element_type=F32
                )
            mixed = (mixed / total).astype(BF)
            for j in range(4):
                mx[g, :, j * HD : (j + 1) * HD] = mixed[j * 64 : (j + 1) * 64]
            m_copy(g).start()

        reshape(0)
        receive(0)
        reshape(1)
        receive(1)
        reshape(2)
        forward(0)
        reshape(3)
        forward(1)
        for b in range(5):
            if b < 2:
                receive(b + 2)
            if b < 4:
                project(b)
            if b < 2:
                forward(b + 2)
            if b >= 1:
                ready(b - 1)
                piece(2 * b - 2, attend)
                piece(2 * b - 1, attend)

    def o_copy(b):
        return copy_to(osend.at[b], orecv.at[b], o_s.at[b], o_r.at[b], mp=beside)

    def y_copy(b):
        return copy_to(ysend.at[b], yrecv.at[b], y_s.at[b], y_r.at[b], mp=across)

    def z_copy(b):
        return copy_to(zsend.at[b], zrecv.at[b], z_s.at[b], z_r.at[b], dp=5 - d)

    def t_copy(b):
        return copy_to(ts.at[b], tr.at[b % 2], t_s.at[b], t_r.at[b % 2], dp=b // 2)

    def t_arrive(p):
        return copy_to(tr.at[p], tr.at[p], t_s.at[0], t_r.at[p], dp=2)

    mine_out = pl.ds(pl.multiple_of((2 * c + y) * 1024, 1024), 1024)

    def u_copy(p):
        return copy_to(us.at[p], fin.at[p, m], u_s.at[p], u_r.at[p], section=s + 1)

    def u_arrive(p):
        return copy_to(fin.at[p, m], fin.at[p, m], u_s.at[p], u_r.at[p], section=s - 1)

    def f_copy(p, k):
        which = across if k == 2 else m
        return copy_to(
            fin.at[p, which],
            fin.at[p, which],
            f_s.at[p, k],
            f_r.at[p, k],
            mp=across if k == 0 else beside,
        )

    def finish(p, total):
        old = h_ref[p * 64 : p * 64 + 64, mine_out].astype(F32)
        us[p] = (old + total).astype(BF)

        @pl.when(s < phases - 1)
        def _():
            u_copy(p).start()

    @pl.when(d >= 2)
    def _():
        @pl.loop(0, 32)
        def _(i):
            part = flat[0, :, pl.ds(pl.multiple_of(i * 65536, 65536), 65536)].astype(F32)
            wo[pl.ds(pl.multiple_of(i * 16, 16), 16), :] = part.reshape(16, 4096).astype(BF)

        def first(b):
            m_arrive(b).wait_recv()
            mine = pl.ds(pl.multiple_of(c * 2048, 2048), 2048)
            other = pl.ds(pl.multiple_of((1 - c) * 2048, 2048), 2048)
            osend[b] = jnp.dot(mr[b], wo[:, other], preferred_element_type=F32).astype(BF)
            o_copy(b).start()
            oown[b] = jnp.dot(mr[b], wo[:, mine], preferred_element_type=F32)

        def second(b):
            o_copy(b).wait_recv()
            mine = pl.ds(pl.multiple_of(y * 1024, 1024), 1024)
            other = pl.ds(pl.multiple_of((1 - y) * 1024, 1024), 1024)
            ysend[b] = (oown[b, :, other] + orecv[b, :, other].astype(F32)).astype(BF)
            y_copy(b).start()
            yown[b] = oown[b, :, mine] + orecv[b, :, mine].astype(F32)

        def third(b):
            y_copy(b).wait_recv()
            keeper = 3 if b >= 6 else 2

            @pl.when(d != keeper)
            def _():
                zsend[b] = (yown[b] + yrecv[b].astype(F32)).astype(BF)
                z_copy(b).start()

            @pl.when(d == keeper)
            def _():
                yown[b] = yown[b] + yrecv[b].astype(F32)

        def fourth(b):
            keeper = 3 if b >= 6 else 2

            @pl.when(d == keeper)
            def _():
                z_copy(b).wait_recv()
                total = yown[b] + zrecv[b].astype(F32)
                if b < 4:
                    ts[b] = total.astype(BF)
                    t_copy(b).start()
                else:
                    finish(b % 2, total)

        for step in range(10):
            for part, stage in ((0, first), (1, third), (2, fourth), (0, second)):
                if 0 <= step - part < 8:
                    piece(step - part, stage)

    @pl.when(d < 2)
    def _():
        def close(p):
            t_arrive(p).wait_recv()
            finish(p, tr[p].astype(F32))

        piece(0, close)
        piece(1, close)

    row = us[1, 48:64, :].astype(F32)[15:16, :]
    squares = jnp.sum(row * row, keepdims=True)
    product = jnp.sum(row * fg_ref[:, mine_out] * rh_ref[:, mine_out], keepdims=True)
    half = lax.broadcasted_iota(jnp.int32, (8, 128), 0) < 4
    st[place] = jnp.where(half, squares, product)

    def st_copy(k):
        t = (place + k) % 16
        return pltpu.make_async_remote_copy(
            src_ref=st.at[place],
            dst_ref=st.at[place],
            send_sem=st_s.at[k - 1],
            recv_sem=st_r.at[k - 1],
            device_id={"dp": t // 4, "mp": t % 4},
            device_id_type=pl.DeviceIdType.MESH,
        )

    def st_arrive(k):
        t = (place + 16 - k) % 16
        return pltpu.make_async_remote_copy(
            src_ref=st.at[t],
            dst_ref=st.at[t],
            send_sem=st_s.at[k - 1],
            recv_sem=st_r.at[k - 1],
            device_id={"dp": t // 4, "mp": t % 4},
            device_id_type=pl.DeviceIdType.MESH,
        )

    def sr_copy(k):
        return copy_to(res, sres, sr_s.at[k - 1], sr_r, section=(s + k) % phases)

    @pl.when(s == phases - 1)
    def _():
        for k in range(1, 16):
            st_copy(k).start()

    @pl.when(s == 0)
    def _():
        out_ref[...] = jnp.zeros_like(out_ref)

    @pl.when(s > 0)
    def _():
        for p in range(2):
            u_arrive(p).wait_recv()
            f_copy(p, 0).start()
            f_copy(p, 1).start()
        for p in range(2):
            f_copy(p, 0).wait_recv()
            f_copy(p, 2).start()

    @pl.when(s == phases - 1)
    def _():
        for k in range(1, 16):
            st_arrive(k).wait_recv()
        for r in range(res.shape[0]):
            end = -1
            for b in range(4):
                end = end + jnp.where(seg_ref[0, b] <= r + 1, 1, 0)
            at_end = jnp.zeros((8, 128), F32)
            for b in range(4):
                block = st[4 * b] + st[4 * b + 1] + st[4 * b + 2] + st[4 * b + 3]
                at_end = at_end + block * jnp.where(end == b, 1.0, 0.0)
            res[r] = at_end
        for k in range(1, phases):
            sr_copy(k).start()
        stat_ref[...] = res[...]

    @pl.when(s > 0)
    def _():
        for p in range(2):
            f_copy(p, 1).wait_recv()
            f_copy(p, 2).wait_recv()
            for k in range(4):
                out_ref[2 * (k % 2) + k // 2, p * 64 : p * 64 + 64] = fin[p, k]
        for p in range(2):
            for k in range(3):
                f_copy(p, k).wait_send()

    @pl.when(s < phases - 1)
    def _():
        sr_copy(1).wait_recv()
        stat_ref[...] = sres[...]
        for p in range(2):
            u_copy(p).wait_send()

    @pl.when(s == phases - 1)
    def _():
        for k in range(1, 16):
            st_copy(k).wait_send()
        for k in range(1, phases):
            sr_copy(k).wait_send()

    for t in range(2):

        @pl.when(d != t)
        def _():
            hop_z(t).wait_send()
            kv_hop(t).wait_send()

    @pl.when(d < 2)
    def _():
        for b in range(4):

            @pl.when(d != b)
            def _():
                for k in range(3):
                    spread(b, k).wait_send()

            q_copy(b).wait_send()
        for g in range(8):
            piece(g, lambda g: m_copy(g).wait_send())

    @pl.when(d >= 2)
    def _():
        def sent(g):
            o_copy(g).wait_send()
            y_copy(g).wait_send()
            keeper = 3 if g >= 6 else 2

            @pl.when(d != keeper)
            def _():
                z_copy(g).wait_send()

            if g < 4:

                @pl.when(d == keeper)
                def _():
                    t_copy(g).wait_send()

        for g in range(8):
            piece(g, sent)


def kept_shards(hidden, norm_gain, kv_weight, attn_flat, final_gain, reward_head, segment_ids, ranks):
    width = hidden.shape[2]
    phases = lax.axis_size("section")
    responses = ranks.shape[0]
    vmem = pl.BlockSpec(memory_space=pltpu.VMEM)
    anywhere = pl.BlockSpec(memory_space=pl.ANY)
    dma = pltpu.SemaphoreType.DMA
    V = pltpu.VMEM
    moved, stats = pl.pallas_call(
        functools.partial(relay_kernel, phases),
        out_shape=(
            jax.ShapeDtypeStruct((4, 128, 1024), BF),
            jax.ShapeDtypeStruct((responses, 8, 128), F32),
        ),
        in_specs=[
            vmem,
            vmem,
            anywhere,
            anywhere,
            pl.BlockSpec(memory_space=pltpu.SMEM),
            vmem,
            vmem,
        ],
        out_specs=(vmem, vmem),
        scratch_shapes=[
            V((4096, 512), BF),
            V((1, 1, 2097152), BF),
            V((2048, 1024), BF),
            V((512, 4096), BF),
            V((128, 4096), BF),
            V((4, 128, 2048), BF),
            V((2, 128, 256), BF),
            V((4, 128, 256), BF),
            V((4, 128, 512), BF),
            V((4, 128, 512), F32),
            V((4, 128, 512), BF),
            V((8, 64, 512), BF),
            V((8, 64, 512), BF),
            V((8, 64, 2048), BF),
            V((8, 64, 2048), F32),
            V((8, 64, 2048), BF),
            V((8, 64, 1024), BF),
            V((8, 64, 1024), F32),
            V((8, 64, 1024), BF),
            V((8, 64, 1024), BF),
            V((8, 64, 1024), BF),
            V((4, 64, 1024), BF),
            V((2, 64, 1024), BF),
            V((2, 64, 1024), BF),
            V((2, 4, 64, 1024), BF),
            V((16, 8, 128), F32),
            V((responses, 8, 128), F32),
            V((responses, 8, 128), F32),
            dma((2,)),
            dma((2,)),
            dma((4,)),
            dma((4, 3)),
            dma((4, 3)),
            dma((2,)),
            dma((4,)),
            dma((4,)),
            dma((4,)),
            dma((8,)),
            dma((8,)),
            dma((8,)),
            dma((8,)),
            dma((8,)),
            dma((8,)),
            dma((8,)),
            dma((8,)),
            dma((4,)),
            dma((2,)),
            dma((2,)),
            dma((2,)),
            dma((2, 3)),
            dma((2, 3)),
            dma((15,)),
            dma((15,)),
            dma((max(phases - 1, 1),)),
            dma(()),
        ],
        compiler_params=pltpu.CompilerParams(
            collective_id=0, has_side_effects=True, vmem_limit_bytes=60 << 20
        ),
    )(
        hidden[0],
        norm_gain,
        kv_weight,
        attn_flat,
        segment_ids,
        final_gain[None],
        reward_head[None],
    )
    rewards = stats[:, 4, 0] * lax.rsqrt(stats[:, 0, 0] / width + EPS)
    pair_loss = jnp.where(
        ranks[:, None] < ranks[None, :], jax.nn.softplus(rewards[None, :] - rewards[:, None]), 0.0
    )
    moved = moved.transpose(1, 0, 2).reshape(1, 128, width)
    return (moved, rewards, pair_loss)


def shards(hidden, norm_gain, kv_weight, attn_flat, final_gain, reward_head, segment_ids, ranks):
    blocks = lax.axis_size("dp")
    lanes = lax.axis_size("mp")
    kv_local = kv_weight.shape[2] // (2 * HD)
    kept = (
        (blocks, lanes, kv_local) == (4, 4, 2)
        and hidden.shape[1:] == (128, 4096)
        and attn_flat.shape == (1, 1, 2097152)
    )
    args = (hidden, norm_gain, kv_weight, attn_flat, final_gain, reward_head, segment_ids, ranks)
    return (kept_shards if kept else gathered_shards)(*args)


def solution(mesh):
    placed = (
        P("section", "dp", None),
        P("section", None),
        P("section", None, "mp"),
        P("section", "mp", "dp"),
        P(),
        P(),
        P("section", None),
        P(),
    )
    return jax.shard_map(
        shards,
        mesh=mesh,
        in_specs=placed,
        out_specs=(P("section", "dp", None), P(), P()),
        check_vma=False,
    )
```

```python
import functools

import jax
import jax.numpy as jnp
from jax import lax
from jax.experimental import pallas as pl
from jax.experimental.pallas import tpu as pltpu
from jax.sharding import PartitionSpec as P

HD = 128
QH = 32
KVH = 8


EPS = 1e-05


def passed_along(block, axis, distance):
    devices = range(lax.axis_size(axis))
    route = [(i - distance, i) for i in devices if i - distance in devices]
    return lax.ppermute(block, axis, route)


def gathered_shards(hidden, norm_gain, kv_weight, attn_flat, final_gain, reward_head, segment_ids, ranks):
    state = hidden[0]
    tokens = state.shape[0]
    width = state.shape[1]
    seg_row = segment_ids[0]
    blocks = lax.axis_size("dp")
    block = lax.axis_index("dp")
    phases = lax.axis_size("section")
    phase_now = lax.axis_index("section")
    responses = ranks.shape[0]
    state_wide = state.astype(jnp.float32)
    normed = (
        state_wide
        * lax.rsqrt(jnp.mean(state_wide * state_wide, -1, keepdims=True) + EPS)
        * norm_gain[0]
    ).astype(jnp.bfloat16)
    keyval = jnp.dot(normed, kv_weight[0], preferred_element_type=jnp.float32).astype(jnp.bfloat16)
    kv_local = keyval.shape[1] // (2 * HD)
    group = QH // KVH
    q_width = kv_local * group * HD
    flat = lax.all_gather(attn_flat[0, 0], "dp", axis=0, tiled=True)
    w_query = flat[: width * q_width].reshape(width, q_width)
    w_out = flat[width * q_width : 2 * width * q_width].reshape(q_width, width)
    query = jnp.dot(normed, w_query, preferred_element_type=jnp.float32).astype(jnp.bfloat16)
    query = query.reshape(tokens, kv_local, group, HD)
    block_ids = jnp.arange(blocks, dtype=jnp.int32)
    own_seg = jnp.sum(jnp.where(block_ids == block, seg_row, 0))
    query_pos = block * tokens + jnp.arange(tokens, dtype=jnp.int32)
    piece = lax.all_gather(keyval, "dp", axis=0, tiled=True)
    peak = jnp.full((kv_local, group, tokens), -1e30, jnp.float32)
    count = piece.shape[0]
    key_pos = jnp.arange(count, dtype=jnp.int32)
    key_block = key_pos // tokens
    key_seg = jnp.sum(jnp.where(key_block[:, None] == block_ids[None, :], seg_row[None, :], 0), 1)
    parts = piece.reshape(count, kv_local, 2, HD)
    keys = parts[:, :, 0]
    values = parts[:, :, 1]
    earlier = (key_block < block) & (key_block >= 0) & ((key_seg == 0) | (key_seg == own_seg))
    same = (key_block == block)[None, :] & (key_pos[None, :] <= query_pos[:, None])
    visible = earlier[None, :] | same
    scores = jnp.einsum("tjgd,cjd->jgtc", query, keys, preferred_element_type=jnp.float32) * HD ** (
        -0.5
    )
    scores = jnp.where(visible[None, None], scores, -1e30)
    new_peak = jnp.maximum(peak, jnp.max(scores, -1))
    weights = jnp.where(visible[None, None], jnp.exp(scores - new_peak[..., None]), 0.0)
    total = jnp.sum(weights, -1)
    accum = jnp.einsum(
        "jgtc,cjd->jgtd", weights.astype(jnp.bfloat16), values, preferred_element_type=jnp.float32
    )
    peak, total, accum = (new_peak, total, accum)
    mixed = (
        (accum / total[..., None])
        .transpose(2, 0, 1, 3)
        .reshape(tokens, q_width)
        .astype(jnp.bfloat16)
    )
    partial_value = jnp.dot(mixed, w_out, preferred_element_type=jnp.float32)
    ends = (
        jnp.sum(
            (seg_row[None, :] <= jnp.arange(1, responses + 1, dtype=jnp.int32)[:, None]).astype(
                jnp.int32
            ),
            1,
        )
        - 1
    )
    at_end = (ends == block) & (phase_now == phases - 1)
    summed = lax.psum(partial_value.astype(jnp.bfloat16), "mp").astype(jnp.float32)
    updated = (state_wide + summed).astype(jnp.bfloat16)
    moved = passed_along(updated, "section", 1)
    last_row = updated[tokens - 1].astype(jnp.float32)
    squares = jnp.sum(last_row * last_row)
    product = jnp.sum(last_row * final_gain * reward_head)
    sums_sq, dots = lax.psum(
        (jnp.where(at_end, squares, 0.0), jnp.where(at_end, product, 0.0)), ("section", "dp")
    )
    rewards = dots * lax.rsqrt(sums_sq / width + EPS)
    pair_loss = jnp.where(
        ranks[:, None] < ranks[None, :], jax.nn.softplus(rewards[None, :] - rewards[:, None]), 0.0
    )
    return (moved[None], rewards, pair_loss)


BF = jnp.bfloat16
F32 = jnp.float32
HIDE = -1e30


def copy_to(src, dst, send, recv, **where):
    return pltpu.make_async_remote_copy(
        src_ref=src,
        dst_ref=dst,
        send_sem=send,
        recv_sem=recv,
        device_id=where,
        device_id_type=pl.DeviceIdType.MESH,
    )


def relay_kernel(
    phases,
    h_ref,
    gain_ref,
    kvw_hbm,
    flat_hbm,
    seg_ref,
    fg_ref,
    rh_ref,
    out_ref,
    stat_ref,
    kvw,
    flat,
    wq,
    wo,
    nrm,
    xq,
    kvs,
    kvr,
    qs,
    qo,
    qr,
    mx,
    mr,
    osend,
    oown,
    orecv,
    ysend,
    yown,
    yrecv,
    zsend,
    zrecv,
    ts,
    tr,
    us,
    fin,
    st,
    res,
    sres,
    load_sem,
    nz_s,
    nz_r,
    nm_s,
    nm_r,
    kv_s,
    kv_r,
    q_s,
    q_r,
    m_s,
    m_r,
    o_s,
    o_r,
    y_s,
    y_r,
    z_s,
    z_r,
    t_s,
    t_r,
    u_s,
    u_r,
    f_s,
    f_r,
    st_s,
    st_r,
    sr_s,
    sr_r,
):
    s = lax.axis_index("section")
    d = lax.axis_index("dp")
    m = lax.axis_index("mp")
    y = m // 2
    c = m % 2
    across = (m + 2) % 4
    beside = m + 1 - 2 * c
    load_kv = pltpu.make_async_copy(kvw_hbm.at[0], kvw, load_sem.at[0])
    load_flat = pltpu.make_async_copy(flat_hbm, flat, load_sem.at[1])
    load_kv.start()
    load_flat.start()

    barrier = pltpu.get_barrier_semaphore()
    place = d * 4 + m
    for k in range(1, 16):
        t = (place + k) % 16
        pl.semaphore_signal(
            barrier,
            inc=1,
            device_id={"dp": t // 4, "mp": t % 4},
            device_id_type=pl.DeviceIdType.MESH,
        )
    for k in range(1, phases):
        pl.semaphore_signal(
            barrier,
            inc=1,
            device_id={"section": (s + k) % phases},
            device_id_type=pl.DeviceIdType.MESH,
        )
    h = h_ref[...].astype(F32)
    scale = lax.rsqrt(jnp.mean(h * h, -1, keepdims=True) + EPS)
    nrm[...] = (h * scale * gain_ref[...]).astype(BF)
    pl.semaphore_wait(barrier, 15 + phases - 1)

    quarter = pl.ds(pl.multiple_of(m * 32, 32), 32)
    far_quarter = pl.ds(pl.multiple_of(across * 32, 32), 32)

    def hop_z(t):
        return copy_to(
            nrm.at[quarter, t * 2048 : (t + 1) * 2048],
            xq.at[d, quarter],
            nz_s.at[t],
            nz_r.at[d],
            dp=t,
        )

    def arrive_z(b):
        return copy_to(xq.at[b, quarter], xq.at[b, quarter], nz_s.at[0], nz_r.at[b], dp=b)

    def spread(b, k):
        rows = far_quarter if k == 2 else quarter
        return copy_to(
            xq.at[b, rows],
            xq.at[b, rows],
            nm_s.at[b, k],
            nm_r.at[b, k],
            mp=across if k == 0 else beside,
        )

    def kv_hop(t):
        return copy_to(kvs.at[t], kvr.at[d], kv_s.at[t], kv_r.at[d], dp=t)

    def kv_arrive(b):
        return copy_to(kvr.at[b], kvr.at[b], kv_s.at[0], kv_r.at[b], dp=b)

    for t in range(2):

        @pl.when(d != t)
        def _():
            hop_z(t).start()

        @pl.when(d == t)
        def _():
            xq[t] = nrm[:, t * 2048 : (t + 1) * 2048]

    load_kv.wait()
    for t in range(2):
        kvs[t] = jnp.dot(
            nrm[...], kvw[:, t * 256 : (t + 1) * 256], preferred_element_type=F32
        ).astype(BF)

        @pl.when(d != t)
        def _():
            kv_hop(t).start()

        @pl.when(d == t)
        def _():
            kvr[t] = kvs[t]

    load_flat.wait()

    def q_copy(b):
        return copy_to(qs.at[b], qr.at[b], q_s.at[b], q_r.at[b], dp=1 - d)

    def m_copy(b):
        return copy_to(mx.at[b], mr.at[b], m_s.at[b], m_r.at[b], dp=d + 2)

    def m_arrive(b):
        return copy_to(mr.at[b], mr.at[b], m_s.at[b], m_r.at[b], dp=d - 2)

    def piece(g, stage):
        if g % 2:
            stage(g)
        else:

            @pl.when(s < phases - 1)
            def _():
                stage(g)

    @pl.when(d < 2)
    def _():
        def reshape(b):
            @pl.loop(0, 8)
            def _(i):
                i = i + b * 8
                part = flat[0, :, pl.ds(pl.multiple_of(i * 65536, 65536), 65536)].astype(F32)
                wq[pl.ds(pl.multiple_of(i * 64, 64), 64), :] = part.reshape(64, 1024).astype(BF)

        def receive(b):
            @pl.when(d != b)
            def _():
                arrive_z(b).wait_recv()
                spread(b, 0).start()
                spread(b, 1).start()

        def forward(b):
            @pl.when(d != b)
            def _():
                spread(b, 0).wait_recv()
                spread(b, 2).start()

        def project(b):
            @pl.when(d != b)
            def _():
                spread(b, 1).wait_recv()
                spread(b, 2).wait_recv()

            mine = pl.ds(pl.multiple_of(d * 512, 512), 512)
            other = pl.ds(pl.multiple_of((1 - d) * 512, 512), 512)
            qs[b] = jnp.dot(xq[b], wq[:, other], preferred_element_type=F32).astype(BF)
            q_copy(b).start()
            qo[b] = jnp.dot(xq[b], wq[:, mine], preferred_element_type=F32)

        def ready(b):
            q_copy(b).wait_recv()

            @pl.when(d != b)
            def _():
                kv_arrive(b).wait_recv()

        def attend(g):
            b, half = g // 2, g % 2
            rows = slice(half * 64, half * 64 + 64)
            q = (qo[b, rows] + qr[b, rows].astype(F32)).astype(BF)
            q = jnp.concatenate([q[:, j * HD : (j + 1) * HD] for j in range(4)], 0)
            scores = []
            for j in range(b + 1):
                score = (
                    lax.dot_general(
                        q, kvr[j, :, :HD], (((1,), (1,)), ((), ())), preferred_element_type=F32
                    )
                    * HD ** (-0.5)
                )
                if j < b:
                    seen = (seg_ref[0, j] == 0) | (seg_ref[0, j] == seg_ref[0, b])
                    score = score + jnp.where(seen, 0.0, HIDE)
                else:
                    row = lax.broadcasted_iota(jnp.int32, score.shape, 0) % 64 + half * 64
                    col = lax.broadcasted_iota(jnp.int32, score.shape, 1)
                    score = jnp.where(col <= row, score, HIDE)
                scores.append(score)
            peak = functools.reduce(jnp.maximum, [jnp.max(x, -1, keepdims=True) for x in scores])
            total = jnp.zeros_like(peak)
            mixed = jnp.zeros((256, HD), F32)
            for j in range(b + 1):
                weight = jnp.exp(scores[j] - peak)
                total = total + jnp.sum(weight, -1, keepdims=True)
                mixed = mixed + jnp.dot(
                    weight.astype(BF), kvr[j, :, HD:], preferred_element_type=F32
                )
            mixed = (mixed / total).astype(BF)
            for j in range(4):
                mx[g, :, j * HD : (j + 1) * HD] = mixed[j * 64 : (j + 1) * 64]
            m_copy(g).start()

        for b in range(3):
            reshape(b)
            receive(b)
        reshape(3)
        forward(0)
        forward(1)
        for b in range(5):
            if b < 4:
                project(b)
            if b == 0:
                receive(3)
            if b < 2:
                forward(b + 2)
            if b >= 1:
                ready(b - 1)
                piece(2 * b - 2, attend)
                piece(2 * b - 1, attend)

    def o_copy(b):
        return copy_to(osend.at[b], orecv.at[b], o_s.at[b], o_r.at[b], mp=beside)

    def y_copy(b):
        return copy_to(ysend.at[b], yrecv.at[b], y_s.at[b], y_r.at[b], mp=across)

    def z_copy(b):
        return copy_to(zsend.at[b], zrecv.at[b], z_s.at[b], z_r.at[b], dp=5 - d)

    def t_copy(b):
        return copy_to(ts.at[b], tr.at[b % 2], t_s.at[b], t_r.at[b % 2], dp=b // 2)

    def t_arrive(p):
        return copy_to(tr.at[p], tr.at[p], t_s.at[0], t_r.at[p], dp=2)

    mine_out = pl.ds(pl.multiple_of((2 * c + y) * 1024, 1024), 1024)

    def u_copy(p):
        return copy_to(us.at[p], fin.at[p, m], u_s.at[p], u_r.at[p], section=s + 1)

    def u_arrive(p):
        return copy_to(fin.at[p, m], fin.at[p, m], u_s.at[p], u_r.at[p], section=s - 1)

    def f_copy(p, k):
        which = across if k == 2 else m
        return copy_to(
            fin.at[p, which],
            fin.at[p, which],
            f_s.at[p, k],
            f_r.at[p, k],
            mp=across if k == 0 else beside,
        )

    def finish(p, total):
        old = h_ref[p * 64 : p * 64 + 64, mine_out].astype(F32)
        us[p] = (old + total).astype(BF)

        @pl.when(s < phases - 1)
        def _():
            u_copy(p).start()

    @pl.when(d >= 2)
    def _():
        @pl.loop(0, 32)
        def _(i):
            part = flat[0, :, pl.ds(pl.multiple_of(i * 65536, 65536), 65536)].astype(F32)
            wo[pl.ds(pl.multiple_of(i * 16, 16), 16), :] = part.reshape(16, 4096).astype(BF)

        def first(b):
            m_arrive(b).wait_recv()
            mine = pl.ds(pl.multiple_of(c * 2048, 2048), 2048)
            other = pl.ds(pl.multiple_of((1 - c) * 2048, 2048), 2048)
            osend[b] = jnp.dot(mr[b], wo[:, other], preferred_element_type=F32).astype(BF)
            o_copy(b).start()
            oown[b] = jnp.dot(mr[b], wo[:, mine], preferred_element_type=F32)

        def second(b):
            o_copy(b).wait_recv()
            mine = pl.ds(pl.multiple_of(y * 1024, 1024), 1024)
            other = pl.ds(pl.multiple_of((1 - y) * 1024, 1024), 1024)
            ysend[b] = (oown[b, :, other] + orecv[b, :, other].astype(F32)).astype(BF)
            y_copy(b).start()
            yown[b] = oown[b, :, mine] + orecv[b, :, mine].astype(F32)

        def third(b):
            y_copy(b).wait_recv()
            keeper = 3 if b >= 6 else 2

            @pl.when(d != keeper)
            def _():
                zsend[b] = (yown[b] + yrecv[b].astype(F32)).astype(BF)
                z_copy(b).start()

            @pl.when(d == keeper)
            def _():
                yown[b] = yown[b] + yrecv[b].astype(F32)

        def fourth(b):
            keeper = 3 if b >= 6 else 2

            @pl.when(d == keeper)
            def _():
                z_copy(b).wait_recv()
                total = yown[b] + zrecv[b].astype(F32)
                if b < 4:
                    ts[b] = total.astype(BF)
                    t_copy(b).start()
                else:
                    finish(b % 2, total)

        for step in range(11):
            for part, stage in ((0, first), (1, second), (2, third), (3, fourth)):
                if 0 <= step - part < 8:
                    piece(step - part, stage)

    @pl.when(d < 2)
    def _():
        def close(p):
            t_arrive(p).wait_recv()
            finish(p, tr[p].astype(F32))

        piece(0, close)
        piece(1, close)

    row = us[1, 48:64, :].astype(F32)[15:16, :]
    squares = jnp.sum(row * row, keepdims=True)
    product = jnp.sum(row * fg_ref[:, mine_out] * rh_ref[:, mine_out], keepdims=True)
    half = lax.broadcasted_iota(jnp.int32, (8, 128), 0) < 4
    st[place] = jnp.where(half, squares, product)

    def st_copy(k):
        t = (place + k) % 16
        return pltpu.make_async_remote_copy(
            src_ref=st.at[place],
            dst_ref=st.at[place],
            send_sem=st_s.at[k - 1],
            recv_sem=st_r.at[k - 1],
            device_id={"dp": t // 4, "mp": t % 4},
            device_id_type=pl.DeviceIdType.MESH,
        )

    def st_arrive(k):
        t = (place + 16 - k) % 16
        return pltpu.make_async_remote_copy(
            src_ref=st.at[t],
            dst_ref=st.at[t],
            send_sem=st_s.at[k - 1],
            recv_sem=st_r.at[k - 1],
            device_id={"dp": t // 4, "mp": t % 4},
            device_id_type=pl.DeviceIdType.MESH,
        )

    def sr_copy(k):
        return copy_to(res, sres, sr_s.at[k - 1], sr_r, section=(s + k) % phases)

    @pl.when(s == phases - 1)
    def _():
        for k in range(1, 16):
            st_copy(k).start()

    @pl.when(s > 0)
    def _():
        for p in range(2):
            u_arrive(p).wait_recv()
            f_copy(p, 0).start()
            f_copy(p, 1).start()
        for p in range(2):
            f_copy(p, 0).wait_recv()
            f_copy(p, 2).start()

    @pl.when(s == phases - 1)
    def _():
        for k in range(1, 16):
            st_arrive(k).wait_recv()
        for r in range(res.shape[0]):
            end = -1
            for b in range(4):
                end = end + jnp.where(seg_ref[0, b] <= r + 1, 1, 0)
            at_end = jnp.zeros((8, 128), F32)
            for b in range(4):
                block = st[4 * b] + st[4 * b + 1] + st[4 * b + 2] + st[4 * b + 3]
                at_end = at_end + block * jnp.where(end == b, 1.0, 0.0)
            res[r] = at_end
        for k in range(1, phases):
            sr_copy(k).start()
        stat_ref[...] = res[...]

    @pl.when(s > 0)
    def _():
        for p in range(2):
            f_copy(p, 1).wait_recv()
            f_copy(p, 2).wait_recv()
            for k in range(4):
                spot = (2 * (k % 2) + k // 2) * 1024
                out_ref[p * 64 : p * 64 + 64, spot : spot + 1024] = fin[p, k]
        for p in range(2):
            for k in range(3):
                f_copy(p, k).wait_send()

    @pl.when(s < phases - 1)
    def _():
        sr_copy(1).wait_recv()
        stat_ref[...] = sres[...]
        for p in range(2):
            u_copy(p).wait_send()

    @pl.when(s == phases - 1)
    def _():
        for k in range(1, 16):
            st_copy(k).wait_send()
        for k in range(1, phases):
            sr_copy(k).wait_send()

    for t in range(2):

        @pl.when(d != t)
        def _():
            hop_z(t).wait_send()
            kv_hop(t).wait_send()

    @pl.when(d < 2)
    def _():
        for b in range(4):

            @pl.when(d != b)
            def _():
                for k in range(3):
                    spread(b, k).wait_send()

            q_copy(b).wait_send()
        for g in range(8):
            piece(g, lambda g: m_copy(g).wait_send())

    @pl.when(d >= 2)
    def _():
        def sent(g):
            o_copy(g).wait_send()
            y_copy(g).wait_send()
            keeper = 3 if g >= 6 else 2

            @pl.when(d != keeper)
            def _():
                z_copy(g).wait_send()

            if g < 4:

                @pl.when(d == keeper)
                def _():
                    t_copy(g).wait_send()

        for g in range(8):
            piece(g, sent)


def kept_shards(hidden, norm_gain, kv_weight, attn_flat, final_gain, reward_head, segment_ids, ranks):
    width = hidden.shape[2]
    phases = lax.axis_size("section")
    responses = ranks.shape[0]
    vmem = pl.BlockSpec(memory_space=pltpu.VMEM)
    anywhere = pl.BlockSpec(memory_space=pl.ANY)
    dma = pltpu.SemaphoreType.DMA
    V = pltpu.VMEM
    moved, stats = pl.pallas_call(
        functools.partial(relay_kernel, phases),
        out_shape=(
            jax.ShapeDtypeStruct((128, 4096), BF),
            jax.ShapeDtypeStruct((responses, 8, 128), F32),
        ),
        in_specs=[
            vmem,
            vmem,
            anywhere,
            anywhere,
            pl.BlockSpec(memory_space=pltpu.SMEM),
            vmem,
            vmem,
        ],
        out_specs=(vmem, vmem),
        scratch_shapes=[
            V((4096, 512), BF),
            V((1, 1, 2097152), BF),
            V((2048, 1024), BF),
            V((512, 4096), BF),
            V((128, 4096), BF),
            V((4, 128, 2048), BF),
            V((2, 128, 256), BF),
            V((4, 128, 256), BF),
            V((4, 128, 512), BF),
            V((4, 128, 512), F32),
            V((4, 128, 512), BF),
            V((8, 64, 512), BF),
            V((8, 64, 512), BF),
            V((8, 64, 2048), BF),
            V((8, 64, 2048), F32),
            V((8, 64, 2048), BF),
            V((8, 64, 1024), BF),
            V((8, 64, 1024), F32),
            V((8, 64, 1024), BF),
            V((8, 64, 1024), BF),
            V((8, 64, 1024), BF),
            V((4, 64, 1024), BF),
            V((2, 64, 1024), BF),
            V((2, 64, 1024), BF),
            V((2, 4, 64, 1024), BF),
            V((16, 8, 128), F32),
            V((responses, 8, 128), F32),
            V((responses, 8, 128), F32),
            dma((2,)),
            dma((2,)),
            dma((4,)),
            dma((4, 3)),
            dma((4, 3)),
            dma((2,)),
            dma((4,)),
            dma((4,)),
            dma((4,)),
            dma((8,)),
            dma((8,)),
            dma((8,)),
            dma((8,)),
            dma((8,)),
            dma((8,)),
            dma((8,)),
            dma((8,)),
            dma((4,)),
            dma((2,)),
            dma((2,)),
            dma((2,)),
            dma((2, 3)),
            dma((2, 3)),
            dma((15,)),
            dma((15,)),
            dma((max(phases - 1, 1),)),
            dma(()),
        ],
        compiler_params=pltpu.CompilerParams(
            collective_id=0, has_side_effects=True, vmem_limit_bytes=60 << 20
        ),
    )(
        hidden[0],
        norm_gain,
        kv_weight,
        attn_flat,
        segment_ids,
        final_gain[None],
        reward_head[None],
    )
    rewards = stats[:, 4, 0] * lax.rsqrt(stats[:, 0, 0] / width + EPS)
    pair_loss = jnp.where(
        ranks[:, None] < ranks[None, :], jax.nn.softplus(rewards[None, :] - rewards[:, None]), 0.0
    )
    moved = jnp.where(lax.axis_index("section") > 0, moved, jnp.zeros_like(moved))
    return (moved[None], rewards, pair_loss)


def shards(hidden, norm_gain, kv_weight, attn_flat, final_gain, reward_head, segment_ids, ranks):
    blocks = lax.axis_size("dp")
    lanes = lax.axis_size("mp")
    kv_local = kv_weight.shape[2] // (2 * HD)
    kept = (
        (blocks, lanes, kv_local) == (4, 4, 2)
        and hidden.shape[1:] == (128, 4096)
        and attn_flat.shape == (1, 1, 2097152)
    )
    args = (hidden, norm_gain, kv_weight, attn_flat, final_gain, reward_head, segment_ids, ranks)
    return (kept_shards if kept else gathered_shards)(*args)


def solution(mesh):
    placed = (
        P("section", "dp", None),
        P("section", None),
        P("section", None, "mp"),
        P("section", "mp", "dp"),
        P(),
        P(),
        P("section", None),
        P(),
    )
    return jax.shard_map(
        shards,
        mesh=mesh,
        in_specs=placed,
        out_specs=(P("section", "dp", None), P(), P()),
        check_vma=False,
    )
```
